512 devices in a mesh: dom: 8 (over z_lo), orb: 64 (over x, y, z_hi, core).
Axes of the slice: x: 4, y: 4, z: 16 (z_hi: 2, z_lo: 8; z = z_hi * 8 + z_lo), core: 2. Of those that a mesh axis runs over, the one named last changes fastest.
Arguments:
- orbitals: float32 [8, 320, 12, 16, 128], P('dom', 'orb'), may hold values from -6 to 6
- potential: float32 [8, 12, 16, 128], P('dom'), may hold values from -3 to 0
- projectors: float32 [16, 8, 512], replicated, may hold values from -0.25 to 0.25
- projector_energy: float32 [8], replicated, may hold values from 20 to 160
- atom_first: int32 [16], replicated, may hold values from 0 to 23
- atom_second: int32 [16], replicated, may hold values from 0 to 31
- atom_third: int32 [16], replicated, may hold values from 0 to 255
- rotation: bfloat16 [320, 320], P('orb'), may hold values from -0.3125 to 0.3125
Outputs:
- rotated: bfloat16 [8, 320, 12, 16, 128], P('dom', 'orb')
The draws below stay inside these ranges and needn't reach their ends.
All inputs are finite; a program needn't handle non-finite values.
Results may differ from the reference program's by a relative error of at most 0.0049.
Values may be sent and summed in bfloat16 or wider, within the bound.
A program may use at most 64 MiB of HBM per device.

```python
import math
import jax
import jax.numpy as jnp
from jax import lax

CX = 12
CY = 16
CZ = 128
NORB = 320
ATOMS = 16
NPROJ = 8
SIDE = 8
SUP = 512
NX = 24
NY = 32
NZ = 256
N_DOM = 8


def place_ends(array, own_key, smallest, top_value):
    extent = array.shape
    index_at = [jax.random.randint(jax.random.fold_in(own_key, axis), (), 0, extent[axis]) for axis in range(len(extent))]
    array = array.at[tuple(index_at)].set(smallest)
    longest = extent.index(max(extent))
    index_at[longest] = (index_at[longest] + 1) % extent[longest]
    return array.at[tuple(index_at)].set(top_value)


def levels(stream_key, extent, cuts, smallest, largest):
    level = 1.0
    for dim, shards_of in cuts:
        steps = jax.random.uniform(jax.random.fold_in(jax.random.fold_in(stream_key, 6), dim), (shards_of,), jnp.float32, smallest / len(cuts), largest / len(cuts))
        level = level * jnp.repeat(jnp.exp(steps), extent[dim] // shards_of).reshape((-1,) + (1,) * (len(extent) - 1 - dim))
    return level


def noise(own_key, shape, scale, limit, shards=(), kind=jnp.bfloat16):
    values = scale * jax.random.normal(own_key, shape, jnp.float32)
    if shards:
        values = values * levels(own_key, shape, shards, -0.22, 0.18)
    return jnp.clip(values, -limit, limit).astype(kind)


def setup_inputs(seed: int = 0) -> dict:
    splits = jax.random.split(jax.random.key(seed), 9)
    orbitals = noise(splits[0], (N_DOM, NORB, CX, CY, CZ), 1.0, 6.0, ((0, 8), (1, 64)), jnp.float32)
    potential = jnp.clip(-3.0 + 3.0 * jax.random.uniform(splits[1], (N_DOM, CX, CY, CZ), jnp.float32) ** levels(splits[1], (N_DOM, CX, CY, CZ), ((0, 8),), -0.2, 0.2), -3.0, 0.0)
    projectors = noise(splits[2], (ATOMS, NPROJ, SUP), SUP ** -0.5, 0.25, (), jnp.float32)
    projector_energy = jnp.clip(jnp.exp(jax.random.uniform(splits[3], (NPROJ,), jnp.float32, math.log(20.0), math.log(160.0))), 20.0, 160.0)
    atom_first = place_ends(jax.random.randint(splits[4], (ATOMS,), 0, NX), jax.random.fold_in(splits[4], 1), 0, NX - 1).astype(jnp.int32)
    atom_second = place_ends(jax.random.randint(splits[5], (ATOMS,), 0, NY), jax.random.fold_in(splits[5], 1), 0, NY - 1).astype(jnp.int32)
    atom_third = place_ends(jax.random.randint(splits[6], (ATOMS,), 0, NZ), jax.random.fold_in(splits[6], 1), 0, NZ - 1).astype(jnp.int32)
    rotation = noise(splits[7], (NORB, NORB), NORB ** -0.5, 0.3125, ((0, 64),))
    return {"orbitals": orbitals, "potential": potential, "projectors": projectors, "projector_energy": projector_energy, "atom_first": atom_first, "atom_second": atom_second, "atom_third": atom_third, "rotation": rotation}


stencil_weights = (-5369.0 / 1800.0, 12.0 / 7.0, -15.0 / 56.0, 10.0 / 189.0, -1.0 / 112.0, 2.0 / 1925.0, -1.0 / 16632.0)
inverse_spacing = 4.0
filter_center = 120.0
filter_width = 110.0


def to_grid(blocks):
    orbital_count = blocks.shape[1]
    stacked = blocks.reshape(NZ // CZ, NY // CY, NX // CX, orbital_count, CX, CY, CZ)
    stacked = stacked.transpose(3, 2, 4, 1, 5, 0, 6)
    return stacked.reshape(orbital_count, NX, NY, NZ)


def to_blocks(grid_values):
    orbital_count = grid_values.shape[0]
    stacked = grid_values.reshape(orbital_count, NX // CX, CX, NY // CY, CY, NZ // CZ, CZ)
    stacked = stacked.transpose(5, 3, 1, 0, 2, 4, 6)
    return stacked.reshape(N_DOM, orbital_count, CX, CY, CZ)


def support_points(atom_first, atom_second, atom_third):
    offsets = jnp.arange(SIDE, dtype=jnp.int32) - SIDE // 2
    coord_first = (atom_first[:, None] + offsets[None, :]) % NX
    coord_second = (atom_second[:, None] + offsets[None, :]) % NY
    coord_third = (atom_third[:, None] + offsets[None, :]) % NZ
    flattened = (coord_first[:, :, None, None] * NY + coord_second[:, None, :, None]) * NZ + coord_third[:, None, None, :]
    return flattened.reshape(ATOMS * SUP).astype(jnp.int32)


def apply_operator(values, local_field, support, projectors, projector_energy):
    summed = 3.0 * stencil_weights[0] * values
    for direction in (1, 2, 3):
        for offset in range(1, 7):
            summed = summed + stencil_weights[offset] * (jnp.roll(values, -offset, direction) + jnp.roll(values, offset, direction))
    orbital_count = values.shape[0]
    flattened = values.reshape(orbital_count, NX * NY * NZ)
    picked = jnp.take(flattened, support, axis=1).reshape(orbital_count, ATOMS, SUP)
    coeffs = jnp.einsum("aps,kas->kap", projectors, picked, precision=lax.Precision.HIGHEST)
    scaled = coeffs * projector_energy[None, None, :]
    spread = jnp.einsum("aps,kap->kas", projectors, scaled, precision=lax.Precision.HIGHEST)
    projected_part = jnp.zeros_like(flattened).at[:, support].add(spread.reshape(orbital_count, ATOMS * SUP))
    kinetic = -0.5 * inverse_spacing * inverse_spacing
    return kinetic * summed + local_field[None] * values + projected_part.reshape(values.shape)


def reference(orbitals, potential, projectors, projector_energy, atom_first, atom_second, atom_third, rotation):
    support = support_points(atom_first, atom_second, atom_third)
    start_values = to_grid(orbitals)
    local_field = to_grid(potential[:, None])[0]
    first_term = (apply_operator(start_values, local_field, support, projectors, projector_energy) - filter_center * start_values) / filter_width
    second_term = 2.0 * (apply_operator(first_term, local_field, support, projectors, projector_energy) - filter_center * first_term) / filter_width - start_values
    filtered = second_term.astype(jnp.bfloat16).reshape(NORB, NX * NY * NZ)
    rotated = jnp.dot(rotation.T, filtered, preferred_element_type=jnp.float32).astype(jnp.bfloat16)
    return to_blocks(rotated.reshape(NORB, NX, NY, NZ))
```

```python
import functools

import jax
import jax.numpy as jnp
import numpy as np
from jax import lax
from jax.experimental import pallas as pl
from jax.experimental.pallas import tpu as pltpu
from jax.sharding import PartitionSpec as P

MESH = pl.DeviceIdType.MESH
F32 = jnp.float32
BF16 = jnp.bfloat16

K, CX, CY, CZ = 5, 12, 16, 128
ROWS = CX * CY
NP = 8
NDOM, NORB_DEV = 8, 64
REACH = 6
WEIGHTS = (
    -5369.0 / 1800.0,
    12.0 / 7.0,
    -15.0 / 56.0,
    10.0 / 189.0,
    -1.0 / 112.0,
    2.0 / 1925.0,
    -1.0 / 16632.0,
)
KINETIC = -8.0
CENTER = 120.0
WIDTH = 110.0


def halves(matrix):
    high = matrix.astype(np.float32).astype(jnp.bfloat16)
    low = (matrix - high.astype(np.float64)).astype(np.float32).astype(jnp.bfloat16)
    return high, low


def hop(distance):
    distance = abs(distance)
    return KINETIC * WEIGHTS[distance] if 1 <= distance <= REACH else 0.0


@functools.cache
def tables():
    own = np.zeros((CX, CY, CX, CY))
    for x in range(CX):
        for y in range(CY):
            for other in range(CX):
                own[x, y, other, y] += hop(x - other)
            for other in range(CY):
                own[x, y, x, other] += hop(y - other)
    own_high, own_low = halves(own.reshape(ROWS, ROWS))
    own3 = np.concatenate((own_high, own_low, own_high), axis=1)

    near = np.zeros((CX, CY, CX, CY))
    for x in range(CX):
        for other in range(CX):
            near[x, np.arange(CY), other, np.arange(CY)] = hop(other + CX - x) + hop(other - CX - x)
    kept = list(range(REACH)) + list(range(CY - REACH, CY))
    side = np.zeros((CX, CY, CX, 2 * REACH))
    pick_y = np.zeros((CX, 2 * REACH, CX, CY))
    for slot, row in enumerate(kept):
        for x in range(CX):
            pick_y[x, slot, x, row] = 1.0
            for y in range(CY):
                side[x, y, x, slot] = hop(row + CY - y) + hop(row - CY - y)
    both = np.concatenate((near.reshape(ROWS, ROWS), side.reshape(ROWS, 12 * CX)), axis=1)
    both_high, both_low = halves(both)
    both2 = np.concatenate((both_high, both_low), axis=1)
    pick_y = pick_y.reshape(12 * CX, ROWS).astype(jnp.bfloat16)

    line = np.array([[hop(z - other) for other in range(CZ)] for z in range(CZ)])
    line_high, line_low = halves(line)
    line3 = np.concatenate((line_high, line_high, line_low), axis=0)

    pick_z = np.zeros((6, CZ, CZ))
    ends = np.zeros((CZ, 6, CZ))
    lanes = list(range(REACH)) + list(range(CZ - REACH, CZ))
    for g in range(6):
        for slot, lane in enumerate(lanes):
            pick_z[g, lane, 12 * g + slot] = 1.0
            for z in range(CZ):
                ends[12 * g + slot, g, z] = hop(lane + CZ - z) + hop(lane - CZ - z)
    ends_high, ends_low = halves(ends.reshape(CZ, 6 * CZ))
    ends2 = np.concatenate((ends_high, ends_low), axis=0)
    pick_z = pick_z.reshape(6 * CZ, CZ).astype(jnp.bfloat16)

    to_tiles = np.zeros((16, 16, 15, 16))
    for q in range(16):
        for m in range(15):
            to_tiles[q, m, m, q] = 1.0
    to_tiles = to_tiles.reshape(256, 240).astype(jnp.bfloat16)
    from_tiles = np.ascontiguousarray(to_tiles.T)

    widen = np.zeros((16, 16, 16, 16))
    for s in range(16):
        for c in range(3):
            for o in range(K):
                for r in range(3):
                    widen[s, 5 * c + o, s, 3 * o + r] = 1.0
    widen = widen.reshape(256, 256).astype(jnp.bfloat16)
    return own3, both2, line3, ends2, pick_y, pick_z, to_tiles, from_tiles, widen


def split(values):
    high = values.astype(BF16)
    low = (values - high.astype(F32)).astype(BF16)
    return high, low


def dot(a, b):
    return jnp.dot(a, b, preferred_element_type=F32)


def exact_dot(a, b):
    return jnp.dot(a, b, preferred_element_type=F32, precision=lax.Precision.HIGHEST)


def kernel(
    first_s, second_s, third_s, energy_s,
    x_ref, v_ref, proj_ref, rot_ref,
    own3, both2, line3, ends2, pick_y, pick_z, to_tiles, from_tiles, widen,
    out_ref,
    turned, across, pxy, szf, y1, acc,
    xsend, ysend, zsend, xrecv, yrecv, zrecv,
    cmsg, crecv, cfull,
    rtmp, rtile, rring, rother, rall,
    rbig, fb, fsend, frecv, gsend, grecv,
    halo_ssem, halo_rsem, c_ssem, c_rsem, ring_ssem, ring_rsem, hand_ssem, hand_rsem, r_ssem, r_rsem, t_ssem, t_rsem,
):
    dom = lax.axis_index("dom")
    orb = lax.axis_index("orb")
    zhi = (orb // 2) % 2
    lane_u = (orb // 4) * 2 + orb % 2

    def plane_peer(i):
        u = (lane_u + i) % 32
        return (dom, (u // 2) * 4 + zhi * 2 + u % 2)

    def dom_peer(i):
        return ((dom + i) % NDOM, orb)

    def ring_peer(step):
        z = (zhi * 8 + dom + step + 16) % 16
        return (z % 8, orb - zhi * 2 + (z // 8) * 2)

    partners = (
        (dom + 1 - 2 * (dom % 2), orb),
        (dom + 2 - 4 * ((dom // 2) % 2), orb),
        (dom + 4 - 8 * (dom // 4), orb),
    )

    barrier = pltpu.get_barrier_semaphore()

    def greet_plane(i, carry):
        pl.semaphore_signal(barrier, inc=1, device_id=plane_peer(i), device_id_type=MESH)
        return carry

    def greet_dom(i, carry):
        pl.semaphore_signal(barrier, inc=1, device_id=dom_peer(i), device_id_type=MESH)
        return carry

    lax.fori_loop(1, NDOM, greet_dom, 0)
    for step in (1, -1):
        pl.semaphore_signal(barrier, inc=1, device_id=ring_peer(step), device_id_type=MESH)
    lax.fori_loop(1, 32, greet_plane, 0)

    lane = lax.broadcasted_iota(jnp.int32, (8, 128), 1)
    sub = lax.broadcasted_iota(jnp.int32, (8, 128), 0)
    first = jnp.zeros((8, 128), jnp.int32)
    second = first
    third = first
    for a in range(16):
        mine = lane // 8 == a
        first = jnp.where(mine, first_s[a], first)
        second = jnp.where(mine, second_s[a], second)
        third = jnp.where(mine, third_s[a], third)
    energy = jnp.zeros((8, 128), F32)
    for p in range(NP):
        energy = jnp.where(sub == p, energy_s[p], energy)
    shift_x = (first - 4 - (dom % 2) * CX + 48) % 24
    shift_y = (second - 4 - (dom // 2 % 2) * CY + 64) % 32
    start_z = (third - 4 - (dom // 4) * CZ + 512) % 256
    cell_z = (start_z + lane % 8) % 256

    swapped = proj_ref[...].T.reshape(64, 8, 128)
    lane3 = lax.broadcasted_iota(jnp.int32, (64, 8, 128), 2)
    sub3 = lax.broadcasted_iota(jnp.int32, (64, 8, 128), 1)
    for bit in (1, 2, 4):
        up = pltpu.roll(pltpu.roll(swapped, 8 - bit, 1), bit, 2)
        down = pltpu.roll(pltpu.roll(swapped, bit, 1), 128 - bit, 2)
        low_s = (sub3 // bit) % 2 == 0
        low_l = (lane3 // bit) % 2 == 0
        swapped = jnp.where(
            jnp.logical_and(low_s, jnp.logical_not(low_l)),
            up,
            jnp.where(jnp.logical_and(jnp.logical_not(low_s), low_l), down, swapped),
        )
    turned[...] = swapped.reshape(512, 128)

    fine = shift_y % 8
    tile_of = jnp.where(sub >= fine, shift_y // 8, (shift_y // 8 + 1) % 4)

    def place_y(i, carry):
        for p in range(NP):
            rows = turned[pl.ds(i * 64 + p, 8, stride=8), :]
            for bit in (1, 2, 4):
                rows = jnp.where((fine // bit) % 2 == 1, pltpu.roll(rows, bit, 0), rows)
            for half_y in range(2):
                across[i, p, pl.ds(8 * half_y, 8), :] = jnp.where(tile_of == half_y, rows, 0.0)
        return carry

    lax.fori_loop(0, 8, place_y, 0)

    def place_x(x, carry):
        hits = [shift_x == (x - i + 24) % 24 for i in range(8)]
        for p in range(NP):
            for half_y in range(2):
                total = jnp.zeros((8, 128), F32)
                for i in range(8):
                    total = jnp.where(hits[i], across[i, p, pl.ds(8 * half_y, 8), :], total)
                pxy[p, pl.ds(x * 16 + 8 * half_y, 8), :] = total
        return carry

    lax.fori_loop(0, CX, place_x, 0)

    zrow = lax.broadcasted_iota(jnp.int32, (128, 128), 0)
    onehot = jnp.where(zrow == jnp.broadcast_to(cell_z[0:1, :], (128, 128)), 1.0, 0.0)
    szf[0] = onehot.astype(BF16)
    szf[1] = onehot.T.astype(BF16)

    lane_128 = lax.broadcasted_iota(jnp.int32, (128, 128), 1)

    def partial_coefficients(source, slot):
        packed = jnp.zeros((8, 128), F32)
        for k in range(K):
            high, low = split(source[k])
            picked = dot(high, szf[0]) + dot(low, szf[0])
            sums = [jnp.sum(picked * pxy[p], axis=0, keepdims=True) for p in range(NP)]
            own = jnp.concatenate(sums, axis=0)
            gather = jnp.where(zrow // 8 + 16 * k == lane_128, 1.0, 0.0)
            packed = packed + exact_dot(own, gather)
        cmsg[slot] = packed
        crecv[slot, dom] = packed

    def send_coefficients(slot):
        copies = []
        for i in range(1, NDOM):
            copies.append(
                pltpu.make_async_remote_copy(
                    src_ref=cmsg.at[slot],
                    dst_ref=crecv.at[slot, dom],
                    send_sem=c_ssem.at[slot],
                    recv_sem=c_rsem.at[slot],
                    device_id=dom_peer(i),
                    device_id_type=MESH,
                )
            )
            copies[-1].start()

    def await_coefficients(slot):
        every = pltpu.make_async_remote_copy(
            src_ref=crecv.at[slot, pl.ds(0, NDOM - 1)],
            dst_ref=crecv.at[slot, pl.ds(0, NDOM - 1)],
            send_sem=c_ssem.at[slot],
            recv_sem=c_rsem.at[slot],
            device_id=dom_peer(1),
            device_id_type=MESH,
        )
        every.wait()
        total = crecv[slot, 0]
        for i in range(1, NDOM):
            total = total + crecv[slot, i]
        total = total * energy
        for k in range(K):
            gather = jnp.where(zrow == lane_128 // 8 + 16 * k, 1.0, 0.0)
            cfull[k] = exact_dot(total, gather)

    def pack_halo(values, level, k):
        high = values.astype(BF16)
        xsend[level, k] = high
        ysend[level, k] = dot(pick_y[...], high).astype(BF16)
        packed = dot(high[0:32], pick_z[0:128, :])
        for g in range(1, 6):
            packed = packed + dot(high[32 * g : 32 * g + 32], pick_z[128 * g : 128 * g + 128, :])
        zsend[level, k] = packed.astype(BF16)

    def halo_copies(level, k):
        pairs = ((zsend, zrecv, 2), (ysend, yrecv, 1), (xsend, xrecv, 0))
        return [
            pltpu.make_async_remote_copy(
                src_ref=source.at[level, k],
                dst_ref=target.at[level, k],
                send_sem=halo_ssem.at[level, axis, k],
                recv_sem=halo_rsem.at[level, axis, k],
                device_id=partners[axis],
                device_id_type=MESH,
            )
            for source, target, axis in pairs
        ]

    def own_part(source, k):
        values = source[k]
        high, low = split(values)
        total = dot(own3[...], jnp.concatenate((high, high, low), axis=0))
        total = total + dot(jnp.concatenate((high, low, high), axis=1), line3[...])
        local = v_ref[...] + (3.0 * KINETIC * WEIGHTS[0] - CENTER)
        acc[k] = total + local * values

    def nonlocal_part(k):
        spread = pxy[0] * cfull[k, 0:1, :]
        for p in range(1, NP):
            spread = spread + pxy[p] * cfull[k, p : p + 1, :]
        high, low = split(spread)
        acc[k] = acc[k] + dot(high, szf[1]) + dot(low, szf[1])

    def halo_part(level, k):
        for copy in halo_copies(level, k):
            copy.wait_recv()
        got = jnp.concatenate((xrecv[level, k], yrecv[level, k]), axis=0)
        total = acc[k] + dot(both2[...], jnp.concatenate((got, got), axis=0))
        zgot = zrecv[level, k]
        ends = dot(jnp.concatenate((zgot, zgot), axis=1), ends2[...])
        flat = jnp.concatenate([ends[:, 128 * g : 128 * g + 128] for g in range(6)], axis=0)
        return total + flat

    partial_coefficients(x_ref, 0)
    for k in range(K):
        pack_halo(x_ref[k], 0, k)
    rtmp[...] = jnp.zeros((16, 128), F32)
    wide = rot_ref[...].astype(F32)
    rtmp[0:5, :] = wide[:, 0:128]
    rtmp[5:10, :] = wide[:, 128:256]
    rtmp[10:15, 0:64] = wide[:, 256:320]
    rtile[...] = rtmp[...].astype(BF16)
    rall[orb] = rtile[...]

    pl.semaphore_wait(barrier, 31 + 7 + 2)
    send_coefficients(0)
    for k in range(K):
        for copy in halo_copies(0, k):
            copy.start()

    def tile_copy(source, i, slot, wave):
        return pltpu.make_async_remote_copy(
            src_ref=source,
            dst_ref=rall.at[slot],
            send_sem=r_ssem.at[wave],
            recv_sem=r_rsem.at[wave],
            device_id=plane_peer(i),
            device_id_type=MESH,
        )

    def send_rows(i, carry):
        tile_copy(rtile, i, orb, 0).start()
        return carry

    lax.fori_loop(1, 32, send_rows, 0)

    for k in range(K):
        own_part(x_ref, k)

    await_coefficients(0)
    ring_copies = []
    for index, step in enumerate((1, -1)):
        ring_copies.append(
            pltpu.make_async_remote_copy(
                src_ref=rtile,
                dst_ref=rring.at[index],
                send_sem=ring_ssem.at[index],
                recv_sem=ring_rsem.at[index],
                device_id=ring_peer(step),
                device_id_type=MESH,
            )
        )
        ring_copies[-1].start()

    for k in range(K):
        nonlocal_part(k)
    for k in range(K):
        y1[k] = halo_part(0, k) * (1.0 / WIDTH)
        pack_halo(y1[k], 1, k)
        if k < 3:
            for copy in halo_copies(1, k):
                copy.start()

    partial_coefficients(y1, 1)
    for copy in ring_copies:
        copy.wait()
    send_coefficients(1)
    hands = [
        pltpu.make_async_remote_copy(
            src_ref=rring.at[1],
            dst_ref=rother,
            send_sem=hand_ssem.at[i],
            recv_sem=hand_rsem,
            device_id=dom_peer(i + 1),
            device_id_type=MESH,
        )
        for i in range(NDOM - 1)
    ]

    @pl.when(dom == NDOM - 1)
    def _():
        for copy in hands:
            copy.start()
        rother[...] = rring[1]

    for k in range(3, K):
        for copy in halo_copies(1, k):
            copy.start()

    for k in range(K):
        own_part(y1, k)

    @pl.when(dom == NDOM - 1)
    def _():
        for copy in hands:
            copy.wait_send()

    @pl.when(dom != NDOM - 1)
    def _():
        hands[0].wait_recv()

    orb_other = orb + 2 - 4 * zhi
    rall[orb_other] = rother[...]

    await_coefficients(1)

    def send_other(i, carry):
        tile_copy(rother, i, orb_other, 1).start()
        return carry

    lax.fori_loop(1, 32, send_other, 0)

    for k in range(K):
        nonlocal_part(k)
    for level in range(2):
        for k in range(K):
            for copy in halo_copies(level, k):
                copy.wait_send()
    for k in range(K):
        fb[k] = (halo_part(1, k) * (2.0 / WIDTH) - x_ref[k]).astype(BF16)
    for g in range(4):
        rows = [fb[o, pl.ds((4 * r + g) * 16, 16), :] for o in range(K) for r in range(3)]
        tiles = dot(to_tiles[...], jnp.concatenate(rows, axis=0))
        fsend[16 * g : 16 * g + 16] = tiles.astype(BF16).reshape(16, 16, 128)

    def exchange(source, target, q, wave):
        return pltpu.make_async_remote_copy(
            src_ref=source,
            dst_ref=target,
            send_sem=t_ssem.at[wave],
            recv_sem=t_rsem.at[wave],
            device_id=(dom, q),
            device_id_type=MESH,
        )

    def send_cells(i, carry):
        q = (orb + i) % NORB_DEV
        exchange(fsend.at[q], frecv.at[orb], q, 0).start()
        return carry

    lax.fori_loop(1, NORB_DEV, send_cells, 0)
    frecv[orb] = fsend[orb]

    for wave in range(2):
        every = tile_copy(rall.at[pl.ds(0, 31)], 1, pl.ds(0, 31), wave)
        every.wait()
    rows_all = rall[...].reshape(1024, 128)
    row_e = lax.broadcasted_iota(jnp.int32, (256, 128), 0)
    lane_e = lax.broadcasted_iota(jnp.int32, (256, 128), 1)
    col_a = lax.broadcasted_iota(jnp.int32, (256, 1024), 1)
    row_b = lax.broadcasted_iota(jnp.int32, (256, 256), 0) % 16
    col_b = lax.broadcasted_iota(jnp.int32, (256, 256), 1) % 16
    same = row_b - 3 * (row_b * 11 // 32) == col_b - 3 * (col_b * 11 // 32)
    third_of = (col_a % 16) * 13 // 64

    def widen_rows(chunk, carry):
        member = row_e % 16
        target = 5 * (chunk * 16 + row_e // 16) + member * 11 // 32
        target = jnp.where(member < 15, target, -1000)
        mixed = jnp.zeros((256, 1024), F32)
        for c in range(3):
            pick = jnp.where(lane_e == target - 128 * c, 1.0, 0.0).astype(BF16)
            part = lax.dot_general(
                pick, rows_all, (((1,), (1,)), ((), ())), preferred_element_type=F32
            )
            mixed = jnp.where(third_of == c, part, mixed)
        mixed = mixed.astype(BF16)
        for s in range(4):
            block = dot(mixed[:, 256 * s : 256 * s + 256], widen[...])
            rbig[pl.ds(chunk * 256, 256), pl.ds(256 * s, 256)] = jnp.where(same, block, 0.0).astype(BF16)
        return carry

    lax.fori_loop(0, 4, widen_rows, 0)

    every = exchange(fsend.at[pl.ds(0, 63)], frecv.at[pl.ds(0, 63)], orb, 0)
    every.wait()
    cells = frecv[...].reshape(1024, 128)
    for i in range(4):
        chunk = (orb // 16 + i) % 4
        turned_cells = dot(rbig[pl.ds(pl.multiple_of(chunk * 256, 256), 256), :], cells)
        gsend[pl.ds(chunk * 16, 16)] = turned_cells.astype(BF16).reshape(16, 16, 128)

        def send_back(j, carry):
            q = chunk * 16 + (orb % 16 + j) % 16
            exchange(gsend.at[q], grecv.at[orb], q, 1).start()
            return carry

        lax.fori_loop(1 if i == 0 else 0, 16, send_back, 0)
    grecv[orb] = gsend[orb]
    every = exchange(gsend.at[pl.ds(0, 63)], grecv.at[pl.ds(0, 63)], orb, 1)
    every.wait()
    for g in range(4):
        rows = dot(from_tiles[...], grecv[16 * g : 16 * g + 16].reshape(256, 128)).astype(BF16)
        for o in range(K):
            for r in range(3):
                m = 3 * o + r
                out_ref[o, pl.ds((4 * r + g) * 16, 16), :] = rows[16 * m : 16 * m + 16]


def body(
    orbitals, potential, projectors, projector_energy, atom_first, atom_second, atom_third, rotation
):
    consts = [jnp.asarray(t) for t in tables()]
    smem = pl.BlockSpec(memory_space=pltpu.SMEM)
    vmem = pl.BlockSpec(memory_space=pltpu.VMEM)
    dma = pltpu.SemaphoreType.DMA
    scratch = [
        pltpu.VMEM((512, 128), F32),
        pltpu.VMEM((8, NP, 16, 128), F32),
        pltpu.VMEM((NP, ROWS, 128), F32),
        pltpu.VMEM((2, 128, 128), BF16),
        pltpu.VMEM((K, ROWS, CZ), F32),
        pltpu.VMEM((K, ROWS, CZ), F32),
        pltpu.VMEM((2, K, ROWS, CZ), BF16),
        pltpu.VMEM((2, K, 144, CZ), BF16),
        pltpu.VMEM((2, K, 32, CZ), BF16),
        pltpu.VMEM((2, K, ROWS, CZ), BF16),
        pltpu.VMEM((2, K, 144, CZ), BF16),
        pltpu.VMEM((2, K, 32, CZ), BF16),
        pltpu.VMEM((2, 8, 128), F32),
        pltpu.VMEM((2, NDOM, 8, 128), F32),
        pltpu.VMEM((K, 8, 128), F32),
        pltpu.VMEM((16, 128), F32),
        pltpu.VMEM((16, 128), BF16),
        pltpu.VMEM((2, 16, 128), BF16),
        pltpu.VMEM((16, 128), BF16),
        pltpu.VMEM((NORB_DEV, 16, 128), BF16),
        pltpu.VMEM((1024, 1024), BF16),
        pltpu.VMEM((K, ROWS, CZ), BF16),
        pltpu.VMEM((NORB_DEV, 16, 128), BF16),
        pltpu.VMEM((NORB_DEV, 16, 128), BF16),
        pltpu.VMEM((NORB_DEV, 16, 128), BF16),
        pltpu.VMEM((NORB_DEV, 16, 128), BF16),
        dma((2, 3, K)),
        dma((2, 3, K)),
        dma((2,)),
        dma((2,)),
        dma((2,)),
        dma((2,)),
        dma((NDOM - 1,)),
        dma(()),
        dma((2,)),
        dma((2,)),
        dma((2,)),
        dma((2,)),
    ]
    result = pl.pallas_call(
        kernel,
        out_shape=jax.ShapeDtypeStruct((K, ROWS, CZ), BF16),
        in_specs=[smem] * 4 + [vmem] * (4 + len(consts)),
        out_specs=vmem,
        scratch_shapes=scratch,
        compiler_params=pltpu.CompilerParams(
            collective_id=0, has_side_effects=True, vmem_limit_bytes=60 << 20
        ),
        name="filter_rotate",
    )(
        atom_first,
        atom_second,
        atom_third,
        projector_energy,
        orbitals.reshape(K, ROWS, CZ),
        potential.reshape(ROWS, CZ),
        projectors.reshape(128, 512),
        rotation,
        *consts,
    )
    return result.reshape((1, K, CX, CY, CZ))


def solution(mesh):
    return jax.shard_map(
        body,
        mesh=mesh,
        in_specs=(
            P("dom", "orb", None, None, None),
            P("dom", None, None, None),
            P(),
            P(),
            P(),
            P(),
            P(),
            P("orb", None),
        ),
        out_specs=P("dom", "orb", None, None, None),
        check_vma=False,
    )
```

```python
import functools

import jax
import jax.numpy as jnp
import numpy as np
from jax import lax
from jax.experimental import pallas as pl
from jax.experimental.pallas import tpu as pltpu
from jax.sharding import PartitionSpec as P

MESH = pl.DeviceIdType.MESH
F32 = jnp.float32
BF16 = jnp.bfloat16

K, CX, CY, CZ = 5, 12, 16, 128
ROWS = CX * CY
NP = 8
NDOM, NORB_DEV = 8, 64
REACH = 6
AHEAD = 2
WEIGHTS = (
    -5369.0 / 1800.0,
    12.0 / 7.0,
    -15.0 / 56.0,
    10.0 / 189.0,
    -1.0 / 112.0,
    2.0 / 1925.0,
    -1.0 / 16632.0,
)
KINETIC = -8.0
CENTER = 120.0
WIDTH = 110.0


def halves(matrix):
    high = matrix.astype(np.float32).astype(jnp.bfloat16)
    low = (matrix - high.astype(np.float64)).astype(np.float32).astype(jnp.bfloat16)
    return high, low


def hop(distance):
    distance = abs(distance)
    return KINETIC * WEIGHTS[distance] if 1 <= distance <= REACH else 0.0


@functools.cache
def tables():
    own = np.zeros((CX, CY, CX, CY))
    for x in range(CX):
        for y in range(CY):
            for other in range(CX):
                own[x, y, other, y] += hop(x - other)
            for other in range(CY):
                own[x, y, x, other] += hop(y - other)
    own_high, own_low = halves(own.reshape(ROWS, ROWS))
    own3 = np.concatenate((own_high, own_low, own_high), axis=1)

    near = np.zeros((CX, CY, CX, CY))
    for x in range(CX):
        for other in range(CX):
            near[x, np.arange(CY), other, np.arange(CY)] = hop(other + CX - x) + hop(other - CX - x)
    kept = list(range(REACH)) + list(range(CY - REACH, CY))
    side = np.zeros((CX, CY, CX, 2 * REACH))
    pick_y = np.zeros((CX, 2 * REACH, CX, CY))
    for slot, row in enumerate(kept):
        for x in range(CX):
            pick_y[x, slot, x, row] = 1.0
            for y in range(CY):
                side[x, y, x, slot] = hop(row + CY - y) + hop(row - CY - y)
    both = np.concatenate((near.reshape(ROWS, ROWS), side.reshape(ROWS, 12 * CX)), axis=1)
    both_high, both_low = halves(both)
    both2 = np.concatenate((both_high, both_low), axis=1)
    pick_y = pick_y.reshape(12 * CX, ROWS).astype(jnp.bfloat16)

    line = np.array([[hop(z - other) for other in range(CZ)] for z in range(CZ)])
    line_high, line_low = halves(line)
    line3 = np.concatenate((line_high, line_high, line_low), axis=0)

    pick_z = np.zeros((6, CZ, CZ))
    ends = np.zeros((CZ, 6, CZ))
    lanes = list(range(REACH)) + list(range(CZ - REACH, CZ))
    for g in range(6):
        for slot, lane in enumerate(lanes):
            pick_z[g, lane, 12 * g + slot] = 1.0
            for z in range(CZ):
                ends[12 * g + slot, g, z] = hop(lane + CZ - z) + hop(lane - CZ - z)
    ends_high, ends_low = halves(ends.reshape(CZ, 6 * CZ))
    ends2 = np.concatenate((ends_high, ends_low), axis=0)
    pick_z = pick_z.reshape(6 * CZ, CZ).astype(jnp.bfloat16)

    to_tiles = np.zeros((16, 16, 15, 16))
    for q in range(16):
        for m in range(15):
            to_tiles[q, m, m, q] = 1.0
    to_tiles = to_tiles.reshape(256, 240).astype(jnp.bfloat16)
    from_tiles = np.ascontiguousarray(to_tiles.T)

    widen = np.zeros((16, 16, 16, 16))
    for s in range(16):
        for c in range(3):
            for o in range(K):
                for r in range(3):
                    widen[s, 5 * c + o, s, 3 * o + r] = 1.0
    widen = widen.reshape(256, 256).astype(jnp.bfloat16)
    return own3, both2, line3, ends2, pick_y, pick_z, to_tiles, from_tiles, widen


def split(values):
    high = values.astype(BF16)
    low = (values - high.astype(F32)).astype(BF16)
    return high, low


def dot(a, b):
    return jnp.dot(a, b, preferred_element_type=F32)


def exact_dot(a, b):
    return jnp.dot(a, b, preferred_element_type=F32, precision=lax.Precision.HIGHEST)


def kernel(
    first_s, second_s, third_s, energy_s,
    x_hbm, v_hbm, proj_hbm, rot_ref,
    own3_hbm, both2_hbm, line3_hbm, ends2_hbm, pick_y_hbm, pick_z_hbm, to_tiles_hbm, from_tiles_hbm, widen_hbm,
    out_ref,
    x_ref, v_ref, proj_ref, own3, both2, line3, ends2, pick_y, pick_z, to_tiles, from_tiles, widen,
    turned, across, pxy, szf, y1, acc,
    xsend, ysend, zsend, xrecv, yrecv, zrecv,
    cmsg, crecv, cfull,
    rtmp, rtile, rring, rother, rall,
    rbig, fb, fsend, frecv, gsend, grecv,
    halo_ssem, halo_rsem, c_ssem, c_rsem, ring_ssem, ring_rsem, hand_ssem, hand_rsem, r_ssem, r_rsem, t_ssem, t_rsem, in_sem,
):
    dom = lax.axis_index("dom")
    orb = lax.axis_index("orb")
    zhi = (orb // 2) % 2
    lane_u = (orb // 4) * 2 + orb % 2

    def plane_peer(i):
        u = (lane_u + i) % 32
        return (dom, (u // 2) * 4 + zhi * 2 + u % 2)

    def dom_peer(i):
        return ((dom + i) % NDOM, orb)

    def ring_peer(step):
        z = (zhi * 8 + dom + step + 16) % 16
        return (z % 8, orb - zhi * 2 + (z // 8) * 2)

    partners = (
        (dom + 1 - 2 * (dom % 2), orb),
        (dom + 2 - 4 * ((dom // 2) % 2), orb),
        (dom + 4 - 8 * (dom // 4), orb),
    )

    barrier = pltpu.get_barrier_semaphore()

    def greet_plane(i, carry):
        pl.semaphore_signal(barrier, inc=1, device_id=plane_peer(i), device_id_type=MESH)
        return carry

    def greet_dom(i, carry):
        pl.semaphore_signal(barrier, inc=1, device_id=dom_peer(i), device_id_type=MESH)
        return carry

    lax.fori_loop(1, NDOM, greet_dom, 0)
    for step in (1, -1):
        pl.semaphore_signal(barrier, inc=1, device_id=ring_peer(step), device_id_type=MESH)
    lax.fori_loop(1, 32, greet_plane, 0)

    inputs = [
        pltpu.make_async_copy(source, target, in_sem.at[index])
        for index, (source, target) in enumerate(
            (
                (proj_hbm, proj_ref),
                (x_hbm, x_ref),
                (pick_y_hbm, pick_y),
                (pick_z_hbm, pick_z),
                (own3_hbm, own3),
                (line3_hbm, line3),
                (v_hbm, v_ref),
                (both2_hbm, both2),
                (ends2_hbm, ends2),
                (widen_hbm, widen),
                (to_tiles_hbm, to_tiles),
                (from_tiles_hbm, from_tiles),
            )
        )
    ]
    for copy in inputs:
        copy.start()

    lane = lax.broadcasted_iota(jnp.int32, (8, 128), 1)
    sub = lax.broadcasted_iota(jnp.int32, (8, 128), 0)
    first = jnp.zeros((8, 128), jnp.int32)
    second = first
    third = first
    for a in range(16):
        mine = lane // 8 == a
        first = jnp.where(mine, first_s[a], first)
        second = jnp.where(mine, second_s[a], second)
        third = jnp.where(mine, third_s[a], third)
    energy = jnp.zeros((8, 128), F32)
    for p in range(NP):
        energy = jnp.where(sub == p, energy_s[p], energy)
    shift_x = (first - 4 - (dom % 2) * CX + 48) % 24
    shift_y = (second - 4 - (dom // 2 % 2) * CY + 64) % 32
    start_z = (third - 4 - (dom // 4) * CZ + 512) % 256
    cell_z = (start_z + lane % 8) % 256

    inputs[0].wait()
    swapped = proj_ref[...].T.reshape(64, 8, 128)
    lane3 = lax.broadcasted_iota(jnp.int32, (64, 8, 128), 2)
    sub3 = lax.broadcasted_iota(jnp.int32, (64, 8, 128), 1)
    for bit in (1, 2, 4):
        up = pltpu.roll(pltpu.roll(swapped, 8 - bit, 1), bit, 2)
        down = pltpu.roll(pltpu.roll(swapped, bit, 1), 128 - bit, 2)
        low_s = (sub3 // bit) % 2 == 0
        low_l = (lane3 // bit) % 2 == 0
        swapped = jnp.where(
            jnp.logical_and(low_s, jnp.logical_not(low_l)),
            up,
            jnp.where(jnp.logical_and(jnp.logical_not(low_s), low_l), down, swapped),
        )
    turned[...] = swapped.reshape(512, 128)

    fine = shift_y % 8
    tile_of = jnp.where(sub >= fine, shift_y // 8, (shift_y // 8 + 1) % 4)

    def place_y(i, carry):
        for p in range(NP):
            rows = turned[pl.ds(i * 64 + p, 8, stride=8), :]
            for bit in (1, 2, 4):
                rows = jnp.where((fine // bit) % 2 == 1, pltpu.roll(rows, bit, 0), rows)
            for half_y in range(2):
                across[i, p, pl.ds(8 * half_y, 8), :] = jnp.where(tile_of == half_y, rows, 0.0)
        return carry

    lax.fori_loop(0, 8, place_y, 0)

    def place_x(x, carry):
        hits = [shift_x == (x - i + 24) % 24 for i in range(8)]
        for p in range(NP):
            for half_y in range(2):
                total = jnp.zeros((8, 128), F32)
                for i in range(8):
                    total = jnp.where(hits[i], across[i, p, pl.ds(8 * half_y, 8), :], total)
                pxy[p, pl.ds(x * 16 + 8 * half_y, 8), :] = total
        return carry

    lax.fori_loop(0, CX, place_x, 0)

    zrow = lax.broadcasted_iota(jnp.int32, (128, 128), 0)
    onehot = jnp.where(zrow == jnp.broadcast_to(cell_z[0:1, :], (128, 128)), 1.0, 0.0)
    szf[0] = onehot.astype(BF16)
    szf[1] = onehot.T.astype(BF16)

    lane_128 = lax.broadcasted_iota(jnp.int32, (128, 128), 1)

    def partial_coefficients(source, k):
        high, low = split(source[k])
        picked = dot(high, szf[0]) + dot(low, szf[0])
        sums = [jnp.sum(picked * pxy[p], axis=0, keepdims=True) for p in range(NP)]
        own = jnp.concatenate(sums, axis=0)
        gather = jnp.where(zrow // 8 + 16 * k == lane_128, 1.0, 0.0)
        return exact_dot(own, gather)

    def hold_coefficients(packed, slot):
        cmsg[slot] = packed
        crecv[slot, dom] = packed

    def send_coefficients(slot):
        copies = []
        for i in range(1, NDOM):
            copies.append(
                pltpu.make_async_remote_copy(
                    src_ref=cmsg.at[slot],
                    dst_ref=crecv.at[slot, dom],
                    send_sem=c_ssem.at[slot],
                    recv_sem=c_rsem.at[slot],
                    device_id=dom_peer(i),
                    device_id_type=MESH,
                )
            )
            copies[-1].start()

    def await_coefficients(slot):
        every = pltpu.make_async_remote_copy(
            src_ref=crecv.at[slot, pl.ds(0, NDOM - 1)],
            dst_ref=crecv.at[slot, pl.ds(0, NDOM - 1)],
            send_sem=c_ssem.at[slot],
            recv_sem=c_rsem.at[slot],
            device_id=dom_peer(1),
            device_id_type=MESH,
        )
        every.wait()
        total = crecv[slot, 0]
        for i in range(1, NDOM):
            total = total + crecv[slot, i]
        total = total * energy
        for k in range(K):
            gather = jnp.where(zrow == lane_128 // 8 + 16 * k, 1.0, 0.0)
            cfull[k] = exact_dot(total, gather)

    def pack_halo(values, level, k):
        high = values.astype(BF16)
        xsend[level, k] = high
        ysend[level, k] = dot(pick_y[...], high).astype(BF16)
        packed = dot(high[0:32], pick_z[0:128, :])
        for g in range(1, 6):
            packed = packed + dot(high[32 * g : 32 * g + 32], pick_z[128 * g : 128 * g + 128, :])
        zsend[level, k] = packed.astype(BF16)

    def halo_copies(level, k):
        pairs = ((zsend, zrecv, 2), (ysend, yrecv, 1), (xsend, xrecv, 0))
        return [
            pltpu.make_async_remote_copy(
                src_ref=source.at[level, k],
                dst_ref=target.at[level, k],
                send_sem=halo_ssem.at[level, axis, k],
                recv_sem=halo_rsem.at[level, axis, k],
                device_id=partners[axis],
                device_id_type=MESH,
            )
            for source, target, axis in pairs
        ]

    def own_part(source, k):
        values = source[k]
        high, low = split(values)
        total = dot(own3[...], jnp.concatenate((high, high, low), axis=0))
        total = total + dot(jnp.concatenate((high, low, high), axis=1), line3[...])
        local = v_ref[...] + (3.0 * KINETIC * WEIGHTS[0] - CENTER)
        acc[k] = total + local * values

    def nonlocal_part(k):
        spread = pxy[0] * cfull[k, 0:1, :]
        for p in range(1, NP):
            spread = spread + pxy[p] * cfull[k, p : p + 1, :]
        high, low = split(spread)
        acc[k] = acc[k] + dot(high, szf[1]) + dot(low, szf[1])

    def halo_part(level, k):
        for copy in halo_copies(level, k):
            copy.wait_recv()
        got = jnp.concatenate((xrecv[level, k], yrecv[level, k]), axis=0)
        total = acc[k] + dot(both2[...], jnp.concatenate((got, got), axis=0))
        zgot = zrecv[level, k]
        ends = dot(jnp.concatenate((zgot, zgot), axis=1), ends2[...])
        flat = jnp.concatenate([ends[:, 128 * g : 128 * g + 128] for g in range(6)], axis=0)
        return total + flat

    inputs[1].wait()
    packed = jnp.zeros((8, 128), F32)
    for k in range(K):
        packed = packed + partial_coefficients(x_ref, k)
    hold_coefficients(packed, 0)
    inputs[2].wait()
    inputs[3].wait()
    for k in range(K):
        pack_halo(x_ref[k], 0, k)
    rtmp[...] = jnp.zeros((16, 128), F32)
    wide = rot_ref[...].astype(F32)
    rtmp[0:5, :] = wide[:, 0:128]
    rtmp[5:10, :] = wide[:, 128:256]
    rtmp[10:15, 0:64] = wide[:, 256:320]
    rtile[...] = rtmp[...].astype(BF16)
    rall[orb] = rtile[...]

    pl.semaphore_wait(barrier, 31 + 7 + 2)
    send_coefficients(0)
    for k in range(K):
        for copy in halo_copies(0, k):
            copy.start()

    def tile_copy(source, i, slot, wave):
        return pltpu.make_async_remote_copy(
            src_ref=source,
            dst_ref=rall.at[slot],
            send_sem=r_ssem.at[wave],
            recv_sem=r_rsem.at[wave],
            device_id=plane_peer(i),
            device_id_type=MESH,
        )

    def send_rows(i, carry):
        tile_copy(rtile, i, orb, 0).start()
        return carry

    lax.fori_loop(1, 32, send_rows, 0)

    for copy in inputs[4:]:
        copy.wait()
    for k in range(K):
        own_part(x_ref, k)

    await_coefficients(0)
    ring_copies = []
    for index, step in enumerate((1, -1)):
        ring_copies.append(
            pltpu.make_async_remote_copy(
                src_ref=rtile,
                dst_ref=rring.at[index],
                send_sem=ring_ssem.at[index],
                recv_sem=ring_rsem.at[index],
                device_id=ring_peer(step),
                device_id_type=MESH,
            )
        )
        ring_copies[-1].start()

    hands = [
        pltpu.make_async_remote_copy(
            src_ref=rring.at[1],
            dst_ref=rother,
            send_sem=hand_ssem.at[i],
            recv_sem=hand_rsem,
            device_id=dom_peer(i + 1),
            device_id_type=MESH,
        )
        for i in range(NDOM - 1)
    ]
    packed = jnp.zeros((8, 128), F32)
    for k in range(K):
        nonlocal_part(k)
        y1[k] = halo_part(0, k) * (1.0 / WIDTH)
        pack_halo(y1[k], 1, k)
        if k < AHEAD:
            for copy in halo_copies(1, k):
                copy.start()
        packed = packed + partial_coefficients(y1, k)
        if k == AHEAD - 1:
            for copy in ring_copies:
                copy.wait()

            @pl.when(dom == NDOM - 1)
            def _():
                for copy in hands:
                    copy.start()
                rother[...] = rring[1]

    hold_coefficients(packed, 1)
    send_coefficients(1)
    for k in range(AHEAD, K):
        for copy in halo_copies(1, k):
            copy.start()

    for k in range(K):
        own_part(y1, k)

    @pl.when(dom == NDOM - 1)
    def _():
        for copy in hands:
            copy.wait_send()

    @pl.when(dom != NDOM - 1)
    def _():
        hands[0].wait_recv()

    orb_other = orb + 2 - 4 * zhi
    rall[orb_other] = rother[...]


    def send_other(i, carry):
        tile_copy(rother, i, orb_other, 1).start()
        return carry

    lax.fori_loop(1, 32, send_other, 0)
    await_coefficients(1)

    for k in range(K):
        nonlocal_part(k)
    for level in range(2):
        for k in range(K):
            for copy in halo_copies(level, k):
                copy.wait_send()
    for k in range(K):
        fb[k] = (halo_part(1, k) * (2.0 / WIDTH) - x_ref[k]).astype(BF16)
    for g in range(4):
        rows = [fb[o, pl.ds((4 * r + g) * 16, 16), :] for o in range(K) for r in range(3)]
        tiles = dot(to_tiles[...], jnp.concatenate(rows, axis=0))
        fsend[16 * g : 16 * g + 16] = tiles.astype(BF16).reshape(16, 16, 128)

    def exchange(source, target, q, wave):
        return pltpu.make_async_remote_copy(
            src_ref=source,
            dst_ref=target,
            send_sem=t_ssem.at[wave],
            recv_sem=t_rsem.at[wave],
            device_id=(dom, q),
            device_id_type=MESH,
        )

    core = orb % 2
    groups = (2 - 2 * zhi + core, 3 - 2 * zhi - core, 2 * zhi + 1 - core, 2 * zhi + core)
    place = orb // 4

    for index, group in enumerate(groups):

        def send_cells(j, carry):
            q = (place + j) % 16 * 4 + group
            exchange(fsend.at[q], frecv.at[orb], q, 0).start()
            return carry

        lax.fori_loop(1 if index == 3 else 0, 16, send_cells, 0)
    frecv[orb] = fsend[orb]

    for wave in range(2):
        every = tile_copy(rall.at[pl.ds(0, 31)], 1, pl.ds(0, 31), wave)
        every.wait()
    rows_all = rall[...].reshape(1024, 128)
    row_e = lax.broadcasted_iota(jnp.int32, (256, 128), 0)
    lane_e = lax.broadcasted_iota(jnp.int32, (256, 128), 1)
    col_a = lax.broadcasted_iota(jnp.int32, (256, 1024), 1)
    row_b = lax.broadcasted_iota(jnp.int32, (256, 256), 0) % 16
    col_b = lax.broadcasted_iota(jnp.int32, (256, 256), 1) % 16
    same = row_b - 3 * (row_b * 11 // 32) == col_b - 3 * (col_b * 11 // 32)
    third_of = (col_a % 16) * 13 // 64

    def widen_rows(chunk, carry):
        member = row_e % 16
        target = 5 * (row_e // 16 * 4 + chunk) + member * 11 // 32
        target = jnp.where(member < 15, target, -1000)
        mixed = jnp.zeros((256, 1024), F32)
        for c in range(3):
            pick = jnp.where(lane_e == target - 128 * c, 1.0, 0.0).astype(BF16)
            part = lax.dot_general(
                pick, rows_all, (((1,), (1,)), ((), ())), preferred_element_type=F32
            )
            mixed = jnp.where(third_of == c, part, mixed)
        mixed = mixed.astype(BF16)
        for s in range(4):
            block = dot(mixed[:, 256 * s : 256 * s + 256], widen[...])
            rbig[pl.ds(chunk * 256, 256), pl.ds(256 * s, 256)] = jnp.where(same, block, 0.0).astype(BF16)
        return carry

    lax.fori_loop(0, 4, widen_rows, 0)

    every = exchange(fsend.at[pl.ds(0, 63)], frecv.at[pl.ds(0, 63)], orb, 0)
    every.wait()
    cells = frecv[...].reshape(1024, 128)
    for index, chunk in enumerate(groups):
        turned_cells = dot(rbig[pl.ds(pl.multiple_of(chunk * 256, 256), 256), :], cells)
        gsend[pl.ds(chunk * 16, 16)] = turned_cells.astype(BF16).reshape(16, 16, 128)

        def send_back(j, carry):
            other = (place + j) % 16
            q = other * 4 + chunk
            exchange(gsend.at[chunk * 16 + other], grecv.at[orb], q, 1).start()
            return carry

        lax.fori_loop(1 if index == 3 else 0, 16, send_back, 0)
    grecv[orb] = gsend[groups[3] * 16 + place]
    every = exchange(gsend.at[pl.ds(0, 63)], grecv.at[pl.ds(0, 63)], orb, 1)
    every.wait()
    for g in range(4):
        rows = dot(from_tiles[...], grecv[16 * g : 16 * g + 16].reshape(256, 128)).astype(BF16)
        for o in range(K):
            for r in range(3):
                m = 3 * o + r
                out_ref[o, pl.ds((4 * r + g) * 16, 16), :] = rows[16 * m : 16 * m + 16]


def body(
    orbitals, potential, projectors, projector_energy, atom_first, atom_second, atom_third, rotation
):
    consts = [jnp.asarray(t) for t in tables()]
    smem = pl.BlockSpec(memory_space=pltpu.SMEM)
    vmem = pl.BlockSpec(memory_space=pltpu.VMEM)
    anywhere = pl.BlockSpec(memory_space=pl.ANY)
    dma = pltpu.SemaphoreType.DMA
    placed = [((K, ROWS, CZ), F32), ((ROWS, CZ), F32), ((128, 512), F32)]
    placed += [(t.shape, BF16) for t in consts]
    scratch = [pltpu.VMEM(shape, kind) for shape, kind in placed] + [
        pltpu.VMEM((512, 128), F32),
        pltpu.VMEM((8, NP, 16, 128), F32),
        pltpu.VMEM((NP, ROWS, 128), F32),
        pltpu.VMEM((2, 128, 128), BF16),
        pltpu.VMEM((K, ROWS, CZ), F32),
        pltpu.VMEM((K, ROWS, CZ), F32),
        pltpu.VMEM((2, K, ROWS, CZ), BF16),
        pltpu.VMEM((2, K, 144, CZ), BF16),
        pltpu.VMEM((2, K, 32, CZ), BF16),
        pltpu.VMEM((2, K, ROWS, CZ), BF16),
        pltpu.VMEM((2, K, 144, CZ), BF16),
        pltpu.VMEM((2, K, 32, CZ), BF16),
        pltpu.VMEM((2, 8, 128), F32),
        pltpu.VMEM((2, NDOM, 8, 128), F32),
        pltpu.VMEM((K, 8, 128), F32),
        pltpu.VMEM((16, 128), F32),
        pltpu.VMEM((16, 128), BF16),
        pltpu.VMEM((2, 16, 128), BF16),
        pltpu.VMEM((16, 128), BF16),
        pltpu.VMEM((NORB_DEV, 16, 128), BF16),
        pltpu.VMEM((1024, 1024), BF16),
        pltpu.VMEM((K, ROWS, CZ), BF16),
        pltpu.VMEM((NORB_DEV, 16, 128), BF16),
        pltpu.VMEM((NORB_DEV, 16, 128), BF16),
        pltpu.VMEM((NORB_DEV, 16, 128), BF16),
        pltpu.VMEM((NORB_DEV, 16, 128), BF16),
        dma((2, 3, K)),
        dma((2, 3, K)),
        dma((2,)),
        dma((2,)),
        dma((2,)),
        dma((2,)),
        dma((NDOM - 1,)),
        dma(()),
        dma((2,)),
        dma((2,)),
        dma((2,)),
        dma((2,)),
        dma((12,)),
    ]
    result = pl.pallas_call(
        kernel,
        out_shape=jax.ShapeDtypeStruct((K, ROWS, CZ), BF16),
        in_specs=[smem] * 4 + [anywhere] * 3 + [vmem] + [anywhere] * len(consts),
        out_specs=vmem,
        scratch_shapes=scratch,
        compiler_params=pltpu.CompilerParams(
            collective_id=0, has_side_effects=True, vmem_limit_bytes=60 << 20
        ),
        name="filter_rotate",
    )(
        atom_first,
        atom_second,
        atom_third,
        projector_energy,
        orbitals.reshape(K, ROWS, CZ),
        potential.reshape(ROWS, CZ),
        projectors.reshape(128, 512),
        rotation,
        *consts,
    )
    return result.reshape((1, K, CX, CY, CZ))


def solution(mesh):
    return jax.shard_map(
        body,
        mesh=mesh,
        in_specs=(
            P("dom", "orb", None, None, None),
            P("dom", None, None, None),
            P(),
            P(),
            P(),
            P(),
            P(),
            P("orb", None),
        ),
        out_specs=P("dom", "orb", None, None, None),
        check_vma=False,
    )
```

```python
import functools

import jax
import jax.numpy as jnp
import numpy as np
from jax import lax
from jax.experimental import pallas as pl
from jax.experimental.pallas import tpu as pltpu
from jax.sharding import PartitionSpec as P

MESH = pl.DeviceIdType.MESH
F32 = jnp.float32
BF16 = jnp.bfloat16

K, CX, CY, CZ = 5, 12, 16, 128
ROWS = CX * CY
NP = 8
NDOM, NORB_DEV = 8, 64
REACH = 6
AHEAD = 1
WEIGHTS = (
    -5369.0 / 1800.0,
    12.0 / 7.0,
    -15.0 / 56.0,
    10.0 / 189.0,
    -1.0 / 112.0,
    2.0 / 1925.0,
    -1.0 / 16632.0,
)
KINETIC = -8.0
CENTER = 120.0
WIDTH = 110.0


def halves(matrix):
    high = matrix.astype(np.float32).astype(jnp.bfloat16)
    low = (matrix - high.astype(np.float64)).astype(np.float32).astype(jnp.bfloat16)
    return high, low


def hop(distance):
    distance = abs(distance)
    return KINETIC * WEIGHTS[distance] if 1 <= distance <= REACH else 0.0


@functools.cache
def tables():
    own = np.zeros((CX, CY, CX, CY))
    for x in range(CX):
        for y in range(CY):
            for other in range(CX):
                own[x, y, other, y] += hop(x - other)
            for other in range(CY):
                own[x, y, x, other] += hop(y - other)
    own_high, own_low = halves(own.reshape(ROWS, ROWS))
    own3 = np.concatenate((own_high, own_low, own_high), axis=1)

    near = np.zeros((CX, CY, CX, CY))
    for x in range(CX):
        for other in range(CX):
            near[x, np.arange(CY), other, np.arange(CY)] = hop(other + CX - x) + hop(other - CX - x)
    kept = list(range(REACH)) + list(range(CY - REACH, CY))
    side = np.zeros((CX, CY, CX, 2 * REACH))
    pick_y = np.zeros((CX, 2 * REACH, CX, CY))
    for slot, row in enumerate(kept):
        for x in range(CX):
            pick_y[x, slot, x, row] = 1.0
            for y in range(CY):
                side[x, y, x, slot] = hop(row + CY - y) + hop(row - CY - y)
    both = np.concatenate((near.reshape(ROWS, ROWS), side.reshape(ROWS, 12 * CX)), axis=1)
    both_high, both_low = halves(both)
    both2 = np.concatenate((both_high, both_low), axis=1)
    pick_y = pick_y.reshape(12 * CX, ROWS).astype(jnp.bfloat16)

    line = np.array([[hop(z - other) for other in range(CZ)] for z in range(CZ)])
    line_high, line_low = halves(line)
    line3 = np.concatenate((line_high, line_high, line_low), axis=0)

    pick_z = np.zeros((6, CZ, CZ))
    ends = np.zeros((CZ, 6, CZ))
    lanes = list(range(REACH)) + list(range(CZ - REACH, CZ))
    for g in range(6):
        for slot, lane in enumerate(lanes):
            pick_z[g, lane, 12 * g + slot] = 1.0
            for z in range(CZ):
                ends[12 * g + slot, g, z] = hop(lane + CZ - z) + hop(lane - CZ - z)
    ends_high, ends_low = halves(ends.reshape(CZ, 6 * CZ))
    ends2 = np.concatenate((ends_high, ends_low), axis=0)
    pick_z = pick_z.reshape(6 * CZ, CZ).astype(jnp.bfloat16)

    to_tiles = np.zeros((16, 16, 15, 16))
    for q in range(16):
        for m in range(15):
            to_tiles[q, m, m, q] = 1.0
    to_tiles = to_tiles.reshape(256, 240).astype(jnp.bfloat16)
    from_tiles = np.ascontiguousarray(to_tiles.T)

    widen = np.zeros((16, 16, 16, 16))
    for s in range(16):
        for c in range(3):
            for o in range(K):
                for r in range(3):
                    widen[s, 5 * c + o, s, 3 * o + r] = 1.0
    widen = widen.reshape(256, 256).astype(jnp.bfloat16)
    join = np.zeros((K, 128, 128))
    for k in range(K):
        for lane in range(128):
            join[k, lane, 16 * k + lane // 8] = 1.0
    part = np.ascontiguousarray(join.transpose(2, 0, 1)).reshape(128, K * 128).astype(jnp.bfloat16)
    join = join.reshape(K * 128, 128).astype(jnp.bfloat16)
    return own3, both2, line3, ends2, pick_y, pick_z, to_tiles, from_tiles, widen, join, part


def split(values):
    high = values.astype(BF16)
    low = (values - high.astype(F32)).astype(BF16)
    return high, low


def dot(a, b):
    return jnp.dot(a, b, preferred_element_type=F32)


def thirds(values):
    high = values.astype(BF16)
    middle, low = split(values - high.astype(F32))
    return jnp.concatenate((high, middle, low), axis=0)


def exact_dot(values, onehot):
    parts = dot(thirds(values), onehot)
    return parts[0:8] + parts[8:16] + parts[16:24]


def kernel(
    first_s, second_s, third_s, energy_s,
    x_hbm, v_hbm, proj_hbm, rot_ref,
    own3_hbm, both2_hbm, line3_hbm, ends2_hbm, pick_y_hbm, pick_z_hbm, to_tiles_hbm, from_tiles_hbm, widen_hbm, join_hbm, part_hbm,
    out_ref,
    x_ref, v_ref, proj_ref, own3, both2, line3, ends2, pick_y, pick_z, to_tiles, from_tiles, widen, join, part,
    turned, across, pxy, szf, y1, acc,
    xsend, ysend, zsend, xrecv, yrecv, zrecv,
    cmsg, crecv, cfull,
    rtmp, rtile, rother, rall,
    rbig, fb, fsend, frecv, gsend, grecv,
    halo_ssem, halo_rsem, c_ssem, c_rsem, ring_ssem, ring_rsem, hand_ssem, hand_rsem, r_ssem, r_rsem, t_ssem, t_rsem, in_sem,
):
    dom = lax.axis_index("dom")
    orb = lax.axis_index("orb")
    zhi = (orb // 2) % 2
    lane_u = (orb // 4) * 2 + orb % 2

    def plane_peer(i):
        u = (lane_u + i) % 32
        return (dom, (u // 2) * 4 + zhi * 2 + u % 2)

    def dom_peer(i):
        return ((dom + i) % NDOM, orb)

    def ring_peer(step):
        z = (zhi * 8 + dom + step + 16) % 16
        return (z % 8, orb - zhi * 2 + (z // 8) * 2)

    partners = (
        (dom + 1 - 2 * (dom % 2), orb),
        (dom + 2 - 4 * ((dom // 2) % 2), orb),
        (dom + 4 - 8 * (dom // 4), orb),
    )

    barrier = pltpu.get_barrier_semaphore()

    def greet_plane(i, carry):
        pl.semaphore_signal(barrier, inc=1, device_id=plane_peer(i), device_id_type=MESH)
        return carry

    def greet_dom(i, carry):
        pl.semaphore_signal(barrier, inc=1, device_id=dom_peer(i), device_id_type=MESH)
        return carry

    lax.fori_loop(1, NDOM, greet_dom, 0)
    for step in (1, -1):
        pl.semaphore_signal(barrier, inc=1, device_id=ring_peer(step), device_id_type=MESH)
    lax.fori_loop(1, 32, greet_plane, 0)

    inputs = [
        pltpu.make_async_copy(source, target, in_sem.at[index])
        for index, (source, target) in enumerate(
            (
                (proj_hbm, proj_ref),
                (x_hbm, x_ref),
                (join_hbm, join),
                (pick_y_hbm, pick_y),
                (pick_z_hbm, pick_z),
                (own3_hbm, own3),
                (line3_hbm, line3),
                (part_hbm, part),
                (v_hbm, v_ref),
                (both2_hbm, both2),
                (ends2_hbm, ends2),
                (widen_hbm, widen),
                (to_tiles_hbm, to_tiles),
                (from_tiles_hbm, from_tiles),
            )
        )
    ]
    for copy in inputs:
        copy.start()

    lane = lax.broadcasted_iota(jnp.int32, (8, 128), 1)
    sub = lax.broadcasted_iota(jnp.int32, (8, 128), 0)
    first = jnp.zeros((8, 128), jnp.int32)
    second = first
    third = first
    for a in range(16):
        mine = lane // 8 == a
        first = jnp.where(mine, first_s[a], first)
        second = jnp.where(mine, second_s[a], second)
        third = jnp.where(mine, third_s[a], third)
    energy = jnp.zeros((8, 128), F32)
    for p in range(NP):
        energy = jnp.where(sub == p, energy_s[p], energy)
    shift_x = (first - 4 - (dom % 2) * CX + 48) % 24
    shift_y = (second - 4 - (dom // 2 % 2) * CY + 64) % 32
    start_z = (third - 4 - (dom // 4) * CZ + 512) % 256
    cell_z = (start_z + lane % 8) % 256

    inputs[0].wait()
    swapped = proj_ref[...].T.reshape(64, 8, 128)
    lane3 = lax.broadcasted_iota(jnp.int32, (64, 8, 128), 2)
    sub3 = lax.broadcasted_iota(jnp.int32, (64, 8, 128), 1)
    for bit in (1, 2, 4):
        up = pltpu.roll(pltpu.roll(swapped, 8 - bit, 1), bit, 2)
        down = pltpu.roll(pltpu.roll(swapped, bit, 1), 128 - bit, 2)
        low_s = (sub3 // bit) % 2 == 0
        low_l = (lane3 // bit) % 2 == 0
        swapped = jnp.where(
            jnp.logical_and(low_s, jnp.logical_not(low_l)),
            up,
            jnp.where(jnp.logical_and(jnp.logical_not(low_s), low_l), down, swapped),
        )
    turned[...] = swapped.reshape(512, 128)

    fine = shift_y % 8
    tile_of = jnp.where(sub >= fine, shift_y // 8, (shift_y // 8 + 1) % 4)

    def place_y(i, carry):
        for p in range(NP):
            rows = turned[pl.ds(i * 64 + p, 8, stride=8), :]
            for bit in (1, 2, 4):
                rows = jnp.where((fine // bit) % 2 == 1, pltpu.roll(rows, bit, 0), rows)
            for half_y in range(2):
                across[i, p, pl.ds(8 * half_y, 8), :] = jnp.where(tile_of == half_y, rows, 0.0)
        return carry

    lax.fori_loop(0, 8, place_y, 0)

    def place_x(x, carry):
        hits = [shift_x == (x - i + 24) % 24 for i in range(8)]
        for p in range(NP):
            for half_y in range(2):
                total = jnp.zeros((8, 128), F32)
                for i in range(8):
                    total = jnp.where(hits[i], across[i, p, pl.ds(8 * half_y, 8), :], total)
                pxy[p, pl.ds(x * 16 + 8 * half_y, 8), :] = total
        return carry

    lax.fori_loop(0, CX, place_x, 0)

    zrow = lax.broadcasted_iota(jnp.int32, (128, 128), 0)
    onehot = jnp.where(zrow == jnp.broadcast_to(cell_z[0:1, :], (128, 128)), 1.0, 0.0)
    szf[0] = onehot.astype(BF16)
    szf[1] = onehot.T.astype(BF16)

    def partial_coefficients(source, k):
        high, low = split(source[k])
        picked = dot(high, szf[0]) + dot(low, szf[0])
        sums = [jnp.sum(picked * pxy[p], axis=0, keepdims=True) for p in range(NP)]
        return jnp.concatenate(sums, axis=0)

    def pack_coefficients(parts):
        return exact_dot(jnp.concatenate(parts, axis=1), join[...])

    def hold_coefficients(packed, slot):
        cmsg[slot] = packed
        crecv[slot, dom] = packed

    def send_coefficients(slot):
        copies = []
        for i in range(1, NDOM):
            copies.append(
                pltpu.make_async_remote_copy(
                    src_ref=cmsg.at[slot],
                    dst_ref=crecv.at[slot, dom],
                    send_sem=c_ssem.at[slot],
                    recv_sem=c_rsem.at[slot],
                    device_id=dom_peer(i),
                    device_id_type=MESH,
                )
            )
            copies[-1].start()

    def await_coefficients(slot):
        every = pltpu.make_async_remote_copy(
            src_ref=crecv.at[slot, pl.ds(0, NDOM - 1)],
            dst_ref=crecv.at[slot, pl.ds(0, NDOM - 1)],
            send_sem=c_ssem.at[slot],
            recv_sem=c_rsem.at[slot],
            device_id=dom_peer(1),
            device_id_type=MESH,
        )
        every.wait()
        total = crecv[slot, 0]
        for i in range(1, NDOM):
            total = total + crecv[slot, i]
        total = total * energy
        spread = exact_dot(total, part[...])
        for k in range(K):
            cfull[k] = spread[:, 128 * k : 128 * k + 128]

    def pack_halo(values, level, k):
        high = values.astype(BF16)
        xsend[level, k] = high
        ysend[level, k] = dot(pick_y[...], high).astype(BF16)
        packed = dot(high[0:32], pick_z[0:128, :])
        for g in range(1, 6):
            packed = packed + dot(high[32 * g : 32 * g + 32], pick_z[128 * g : 128 * g + 128, :])
        zsend[level, k] = packed.astype(BF16)

    def halo_copies(level, k):
        pairs = ((zsend, zrecv, 2), (ysend, yrecv, 1), (xsend, xrecv, 0))
        return [
            pltpu.make_async_remote_copy(
                src_ref=source.at[level, k],
                dst_ref=target.at[level, k],
                send_sem=halo_ssem.at[level, axis, k],
                recv_sem=halo_rsem.at[level, axis, k],
                device_id=partners[axis],
                device_id_type=MESH,
            )
            for source, target, axis in pairs
        ]

    def own_part(source, k):
        values = source[k]
        high, low = split(values)
        total = dot(own3[...], jnp.concatenate((high, high, low), axis=0))
        total = total + dot(jnp.concatenate((high, low, high), axis=1), line3[...])
        local = v_ref[...] + (3.0 * KINETIC * WEIGHTS[0] - CENTER)
        acc[k] = total + local * values

    def nonlocal_part(k):
        spread = pxy[0] * cfull[k, 0:1, :]
        for p in range(1, NP):
            spread = spread + pxy[p] * cfull[k, p : p + 1, :]
        high, low = split(spread)
        acc[k] = acc[k] + dot(high, szf[1]) + dot(low, szf[1])

    def halo_part(level, k):
        for copy in halo_copies(level, k):
            copy.wait_recv()
        got = jnp.concatenate((xrecv[level, k], yrecv[level, k]), axis=0)
        total = acc[k] + dot(both2[...], jnp.concatenate((got, got), axis=0))
        zgot = zrecv[level, k]
        ends = dot(jnp.concatenate((zgot, zgot), axis=1), ends2[...])
        flat = jnp.concatenate([ends[:, 128 * g : 128 * g + 128] for g in range(6)], axis=0)
        return total + flat

    inputs[1].wait()
    inputs[2].wait()
    parts = []
    high, low = split(x_ref[...].reshape(K * ROWS, CZ))
    picked = (dot(high, szf[0]) + dot(low, szf[0])).reshape(K, ROWS, CZ)
    for k in range(K):
        sums = [jnp.sum(picked[k] * pxy[p], axis=0, keepdims=True) for p in range(NP)]
        parts.append(jnp.concatenate(sums, axis=0))
    hold_coefficients(pack_coefficients(parts), 0)
    inputs[3].wait()
    inputs[4].wait()
    for k in range(K):
        pack_halo(x_ref[k], 0, k)
    rtmp[...] = jnp.zeros((16, 128), F32)
    wide = rot_ref[...].astype(F32)
    rtmp[0:5, :] = wide[:, 0:128]
    rtmp[5:10, :] = wide[:, 128:256]
    rtmp[10:15, 0:64] = wide[:, 256:320]
    rtile[...] = rtmp[...].astype(BF16)
    rall[orb] = rtile[...]

    pl.semaphore_wait(barrier, 31 + 7 + 2)
    send_coefficients(0)

    ring_copy = pltpu.make_async_remote_copy(
        src_ref=rtile,
        dst_ref=rother,
        send_sem=ring_ssem,
        recv_sem=ring_rsem,
        device_id=ring_peer(-1),
        device_id_type=MESH,
    )
    hands = [
        pltpu.make_async_remote_copy(
            src_ref=rother,
            dst_ref=rother,
            send_sem=hand_ssem.at[i],
            recv_sem=hand_rsem,
            device_id=dom_peer(i + 1),
            device_id_type=MESH,
        )
        for i in range(NDOM - 1)
    ]

    @pl.when(dom == 0)
    def _():
        ring_copy.start()

    for k in range(2):
        for copy in halo_copies(0, k):
            copy.start()

    def tile_copy(source, i, slot, wave):
        return pltpu.make_async_remote_copy(
            src_ref=source,
            dst_ref=rall.at[slot],
            send_sem=r_ssem.at[wave],
            recv_sem=r_rsem.at[wave],
            device_id=plane_peer(i),
            device_id_type=MESH,
        )

    def send_rows(i, carry):
        tile_copy(rtile, i, orb, 0).start()
        return carry

    lax.fori_loop(1, 32, send_rows, 0)

    @pl.when(dom == NDOM - 1)
    def _():
        ring_copy.wait_recv()
        for copy in hands:
            copy.start()

    for copy in inputs[5:]:
        copy.wait()
    for k in range(K):
        own_part(x_ref, k)
        if k + 2 < K:
            for copy in halo_copies(0, k):
                copy.wait_send()
            for copy in halo_copies(0, k + 2):
                copy.start()

    await_coefficients(0)

    @pl.when(dom == 0)
    def _():
        ring_copy.wait_send()

    @pl.when(dom == NDOM - 1)
    def _():
        for copy in hands:
            copy.wait_send()

    @pl.when(dom != NDOM - 1)
    def _():
        hands[0].wait_recv()

    orb_other = orb + 2 - 4 * zhi
    rall[orb_other] = rother[...]

    def send_other(i, carry):
        tile_copy(rother, i, orb_other, 1).start()
        return carry

    lax.fori_loop(1, 32, send_other, 0)

    parts = []
    for k in range(K):
        nonlocal_part(k)
        y1[k] = halo_part(0, k) * (1.0 / WIDTH)
        pack_halo(y1[k], 1, k)
        if k < AHEAD:
            for copy in halo_copies(1, k):
                copy.start()
        parts.append(partial_coefficients(y1, k))

    hold_coefficients(pack_coefficients(parts), 1)
    send_coefficients(1)
    for k in range(AHEAD, K):
        for copy in halo_copies(1, k):
            copy.start()

    for k in range(K):
        own_part(y1, k)

    await_coefficients(1)

    for k in range(K):
        nonlocal_part(k)
    for level in range(2):
        for k in range(K - 2 if level == 0 else 0, K):
            for copy in halo_copies(level, k):
                copy.wait_send()
    for k in range(K):
        fb[k] = (halo_part(1, k) * (2.0 / WIDTH) - x_ref[k]).astype(BF16)
    for g in range(4):
        rows = [fb[o, pl.ds((4 * r + g) * 16, 16), :] for o in range(K) for r in range(3)]
        tiles = dot(to_tiles[...], jnp.concatenate(rows, axis=0))
        fsend[16 * g : 16 * g + 16] = tiles.astype(BF16).reshape(16, 16, 128)

    for wave in range(2):
        every = tile_copy(rall.at[pl.ds(0, 31)], 1, pl.ds(0, 31), wave)
        every.wait()

    def exchange(source, target, q, wave):
        return pltpu.make_async_remote_copy(
            src_ref=source,
            dst_ref=target,
            send_sem=t_ssem.at[wave],
            recv_sem=t_rsem.at[wave],
            device_id=(dom, q),
            device_id_type=MESH,
        )

    core = orb % 2
    groups = (2 - 2 * zhi + core, 3 - 2 * zhi - core, 2 * zhi + 1 - core, 2 * zhi + core)
    place = orb // 4

    for index, group in enumerate(groups):

        def send_cells(j, carry):
            q = (place + j) % 16 * 4 + group
            exchange(fsend.at[q], frecv.at[orb], q, 0).start()
            return carry

        lax.fori_loop(1 if index == 3 else 0, 16, send_cells, 0)
    frecv[orb] = fsend[orb]

    rows_all = rall[...].reshape(1024, 128)
    row_e = lax.broadcasted_iota(jnp.int32, (256, 128), 0)
    lane_e = lax.broadcasted_iota(jnp.int32, (256, 128), 1)
    col_a = lax.broadcasted_iota(jnp.int32, (256, 1024), 1)
    row_b = lax.broadcasted_iota(jnp.int32, (256, 256), 0) % 16
    col_b = lax.broadcasted_iota(jnp.int32, (256, 256), 1) % 16
    same = row_b - 3 * (row_b * 11 // 32) == col_b - 3 * (col_b * 11 // 32)
    third_of = (col_a % 16) * 13 // 64

    def widen_rows(chunk, carry):
        member = row_e % 16
        target = 5 * (row_e // 16 * 4 + chunk) + member * 11 // 32
        target = jnp.where(member < 15, target, -1000)
        mixed = jnp.zeros((256, 1024), F32)
        for c in range(3):
            pick = jnp.where(lane_e == target - 128 * c, 1.0, 0.0).astype(BF16)
            part = lax.dot_general(
                pick, rows_all, (((1,), (1,)), ((), ())), preferred_element_type=F32
            )
            mixed = jnp.where(third_of == c, part, mixed)
        mixed = mixed.astype(BF16)
        for s in range(4):
            block = dot(mixed[:, 256 * s : 256 * s + 256], widen[...])
            rbig[pl.ds(chunk * 256, 256), pl.ds(256 * s, 256)] = jnp.where(same, block, 0.0).astype(BF16)
        return carry

    lax.fori_loop(0, 4, widen_rows, 0)

    every = exchange(fsend.at[pl.ds(0, 63)], frecv.at[pl.ds(0, 63)], orb, 0)
    every.wait()
    cells = frecv[...].reshape(1024, 128)
    for index, chunk in enumerate(groups):
        turned_cells = dot(rbig[pl.ds(pl.multiple_of(chunk * 256, 256), 256), :], cells)
        gsend[pl.ds(chunk * 16, 16)] = turned_cells.astype(BF16).reshape(16, 16, 128)

        def send_back(j, carry):
            other = (place + j) % 16
            q = other * 4 + chunk
            exchange(gsend.at[chunk * 16 + other], grecv.at[orb], q, 1).start()
            return carry

        lax.fori_loop(1 if index == 3 else 0, 16, send_back, 0)
    grecv[orb] = gsend[groups[3] * 16 + place]
    every = exchange(gsend.at[pl.ds(0, 63)], grecv.at[pl.ds(0, 63)], orb, 1)
    every.wait()
    for g in range(4):
        rows = dot(from_tiles[...], grecv[16 * g : 16 * g + 16].reshape(256, 128)).astype(BF16)
        for o in range(K):
            for r in range(3):
                m = 3 * o + r
                out_ref[o, pl.ds((4 * r + g) * 16, 16), :] = rows[16 * m : 16 * m + 16]


def body(
    orbitals, potential, projectors, projector_energy, atom_first, atom_second, atom_third, rotation
):
    consts = [jnp.asarray(t) for t in tables()]
    smem = pl.BlockSpec(memory_space=pltpu.SMEM)
    vmem = pl.BlockSpec(memory_space=pltpu.VMEM)
    anywhere = pl.BlockSpec(memory_space=pl.ANY)
    dma = pltpu.SemaphoreType.DMA
    placed = [((K, ROWS, CZ), F32), ((ROWS, CZ), F32), ((128, 512), F32)]
    placed += [(t.shape, BF16) for t in consts]
    scratch = [pltpu.VMEM(shape, kind) for shape, kind in placed] + [
        pltpu.VMEM((512, 128), F32),
        pltpu.VMEM((8, NP, 16, 128), F32),
        pltpu.VMEM((NP, ROWS, 128), F32),
        pltpu.VMEM((2, 128, 128), BF16),
        pltpu.VMEM((K, ROWS, CZ), F32),
        pltpu.VMEM((K, ROWS, CZ), F32),
        pltpu.VMEM((2, K, ROWS, CZ), BF16),
        pltpu.VMEM((2, K, 144, CZ), BF16),
        pltpu.VMEM((2, K, 32, CZ), BF16),
        pltpu.VMEM((2, K, ROWS, CZ), BF16),
        pltpu.VMEM((2, K, 144, CZ), BF16),
        pltpu.VMEM((2, K, 32, CZ), BF16),
        pltpu.VMEM((2, 8, 128), F32),
        pltpu.VMEM((2, NDOM, 8, 128), F32),
        pltpu.VMEM((K, 8, 128), F32),
        pltpu.VMEM((16, 128), F32),
        pltpu.VMEM((16, 128), BF16),
        pltpu.VMEM((16, 128), BF16),
        pltpu.VMEM((NORB_DEV, 16, 128), BF16),
        pltpu.VMEM((1024, 1024), BF16),
        pltpu.VMEM((K, ROWS, CZ), BF16),
        pltpu.VMEM((NORB_DEV, 16, 128), BF16),
        pltpu.VMEM((NORB_DEV, 16, 128), BF16),
        pltpu.VMEM((NORB_DEV, 16, 128), BF16),
        pltpu.VMEM((NORB_DEV, 16, 128), BF16),
        dma((2, 3, K)),
        dma((2, 3, K)),
        dma((2,)),
        dma((2,)),
        dma(()),
        dma(()),
        dma((NDOM - 1,)),
        dma(()),
        dma((2,)),
        dma((2,)),
        dma((2,)),
        dma((2,)),
        dma((14,)),
    ]
    result = pl.pallas_call(
        kernel,
        out_shape=jax.ShapeDtypeStruct((K, ROWS, CZ), BF16),
        in_specs=[smem] * 4 + [anywhere] * 3 + [vmem] + [anywhere] * len(consts),
        out_specs=vmem,
        scratch_shapes=scratch,
        compiler_params=pltpu.CompilerParams(
            collective_id=0, has_side_effects=True, vmem_limit_bytes=60 << 20
        ),
        name="filter_rotate",
    )(
        atom_first,
        atom_second,
        atom_third,
        projector_energy,
        orbitals.reshape(K, ROWS, CZ),
        potential.reshape(ROWS, CZ),
        projectors.reshape(128, 512),
        rotation,
        *consts,
    )
    return result.reshape((1, K, CX, CY, CZ))


def solution(mesh):
    return jax.shard_map(
        body,
        mesh=mesh,
        in_specs=(
            P("dom", "orb", None, None, None),
            P("dom", None, None, None),
            P(),
            P(),
            P(),
            P(),
            P(),
            P("orb", None),
        ),
        out_specs=P("dom", "orb", None, None, None),
        check_vma=False,
    )
```

```python
import functools

import jax
import jax.numpy as jnp
import numpy as np
from jax import lax
from jax.experimental import pallas as pl
from jax.experimental.pallas import tpu as pltpu
from jax.sharding import PartitionSpec as P

MESH = pl.DeviceIdType.MESH
F32 = jnp.float32
BF16 = jnp.bfloat16

K, CX, CY, CZ = 5, 12, 16, 128
ROWS = CX * CY
NP = 8
NDOM, NORB_DEV = 8, 64
REACH = 6
AHEAD = 1
WEIGHTS = (
    -5369.0 / 1800.0,
    12.0 / 7.0,
    -15.0 / 56.0,
    10.0 / 189.0,
    -1.0 / 112.0,
    2.0 / 1925.0,
    -1.0 / 16632.0,
)
KINETIC = -8.0
CENTER = 120.0
WIDTH = 110.0


def halves(matrix):
    high = matrix.astype(np.float32).astype(jnp.bfloat16)
    low = (matrix - high.astype(np.float64)).astype(np.float32).astype(jnp.bfloat16)
    return high, low


def hop(distance):
    distance = abs(distance)
    return KINETIC * WEIGHTS[distance] if 1 <= distance <= REACH else 0.0


@functools.cache
def tables():
    own = np.zeros((CX, CY, CX, CY))
    for x in range(CX):
        for y in range(CY):
            for other in range(CX):
                own[x, y, other, y] += hop(x - other)
            for other in range(CY):
                own[x, y, x, other] += hop(y - other)
    own_high, own_low = halves(own.reshape(ROWS, ROWS))
    own3 = np.concatenate((own_high, own_low, own_high), axis=1)

    near = np.zeros((CX, CY, CX, CY))
    for x in range(CX):
        for other in range(CX):
            near[x, np.arange(CY), other, np.arange(CY)] = hop(other + CX - x) + hop(other - CX - x)
    kept = list(range(REACH)) + list(range(CY - REACH, CY))
    side = np.zeros((CX, CY, CX, 2 * REACH))
    pick_y = np.zeros((CX, 2 * REACH, CX, CY))
    for slot, row in enumerate(kept):
        for x in range(CX):
            pick_y[x, slot, x, row] = 1.0
            for y in range(CY):
                side[x, y, x, slot] = hop(row + CY - y) + hop(row - CY - y)
    both = np.concatenate((near.reshape(ROWS, ROWS), side.reshape(ROWS, 12 * CX)), axis=1)
    both_high, both_low = halves(both)
    both2 = np.concatenate((both_high, both_low), axis=1)
    pick_y = pick_y.reshape(12 * CX, ROWS).astype(jnp.bfloat16)

    line = np.array([[hop(z - other) for other in range(CZ)] for z in range(CZ)])
    line_high, line_low = halves(line)
    line3 = np.concatenate((line_high, line_high, line_low), axis=0)

    pick_z = np.zeros((6, CZ, CZ))
    ends = np.zeros((CZ, 6, CZ))
    lanes = list(range(REACH)) + list(range(CZ - REACH, CZ))
    for g in range(6):
        for slot, lane in enumerate(lanes):
            pick_z[g, lane, 12 * g + slot] = 1.0
            for z in range(CZ):
                ends[12 * g + slot, g, z] = hop(lane + CZ - z) + hop(lane - CZ - z)
    ends_high, ends_low = halves(ends.reshape(CZ, 6 * CZ))
    ends2 = np.concatenate((ends_high, ends_low), axis=0)
    pick_z = pick_z.reshape(6 * CZ, CZ).astype(jnp.bfloat16)

    to_tiles = np.zeros((16, 16, 15, 16))
    for q in range(16):
        for m in range(15):
            to_tiles[q, m, m, q] = 1.0
    to_tiles = to_tiles.reshape(256, 240).astype(jnp.bfloat16)
    from_tiles = np.ascontiguousarray(to_tiles.T)

    widen = np.zeros((16, 16, 16, 16))
    for s in range(16):
        for c in range(3):
            for o in range(K):
                for r in range(3):
                    widen[s, 5 * c + o, s, 3 * o + r] = 1.0
    widen = widen.reshape(256, 256).astype(jnp.bfloat16)
    join = np.zeros((K, 128, 128))
    for k in range(K):
        for lane in range(128):
            join[k, lane, 16 * k + lane // 8] = 1.0
    part = np.ascontiguousarray(join.transpose(2, 0, 1)).reshape(128, K * 128).astype(jnp.bfloat16)
    join = join.reshape(K * 128, 128).astype(jnp.bfloat16)
    return own3, both2, line3, ends2, pick_y, pick_z, to_tiles, from_tiles, widen, join, part


def split(values):
    high = values.astype(BF16)
    low = (values - high.astype(F32)).astype(BF16)
    return high, low


def dot(a, b):
    return jnp.dot(a, b, preferred_element_type=F32)


def thirds(values):
    high = values.astype(BF16)
    middle, low = split(values - high.astype(F32))
    return jnp.concatenate((high, middle, low), axis=0)


def exact_dot(values, onehot):
    parts = dot(thirds(values), onehot)
    return parts[0:8] + parts[8:16] + parts[16:24]


def kernel(
    first_s, second_s, third_s, energy_s,
    x_hbm, v_hbm, proj_hbm, rot_ref,
    own3_hbm, both2_hbm, line3_hbm, ends2_hbm, pick_y_hbm, pick_z_hbm, to_tiles_hbm, from_tiles_hbm, widen_hbm, join_hbm, part_hbm,
    out_ref,
    x_ref, v_ref, proj_ref, own3, both2, line3, ends2, pick_y, pick_z, to_tiles, from_tiles, widen, join, part,
    turned, across, pxy, szf, y1, acc,
    xsend, ysend, zsend, xrecv, yrecv, zrecv,
    cmsg, crecv, cfull,
    rtmp, rtile, rother, rall,
    rbig, fb, fsend, frecv, gsend, grecv,
    halo_ssem, halo_rsem, c_ssem, c_rsem, ring_ssem, ring_rsem, hand_ssem, hand_rsem, r_ssem, r_rsem, t_ssem, t_rsem, in_sem,
):
    dom = lax.axis_index("dom")
    orb = lax.axis_index("orb")
    zhi = (orb // 2) % 2
    lane_u = (orb // 4) * 2 + orb % 2

    def plane_peer(i):
        u = (lane_u + i) % 32
        return (dom, (u // 2) * 4 + zhi * 2 + u % 2)

    def dom_peer(i):
        return ((dom + i) % NDOM, orb)

    def ring_peer(step):
        z = (zhi * 8 + dom + step + 16) % 16
        return (z % 8, orb - zhi * 2 + (z // 8) * 2)

    partners = (
        (dom + 1 - 2 * (dom % 2), orb),
        (dom + 2 - 4 * ((dom // 2) % 2), orb),
        (dom + 4 - 8 * (dom // 4), orb),
    )

    barrier = pltpu.get_barrier_semaphore()

    def greet_plane(i, carry):
        pl.semaphore_signal(barrier, inc=1, device_id=plane_peer(i), device_id_type=MESH)
        return carry

    def greet_dom(i, carry):
        pl.semaphore_signal(barrier, inc=1, device_id=dom_peer(i), device_id_type=MESH)
        return carry

    lax.fori_loop(1, NDOM, greet_dom, 0)
    for step in (1, -1):
        pl.semaphore_signal(barrier, inc=1, device_id=ring_peer(step), device_id_type=MESH)
    lax.fori_loop(1, 32, greet_plane, 0)

    inputs = [
        pltpu.make_async_copy(source, target, in_sem.at[index])
        for index, (source, target) in enumerate(
            (
                (proj_hbm, proj_ref),
                (x_hbm, x_ref),
                (join_hbm, join),
                (pick_y_hbm, pick_y),
                (pick_z_hbm, pick_z),
                (own3_hbm, own3),
                (line3_hbm, line3),
                (part_hbm, part),
                (v_hbm, v_ref),
                (both2_hbm, both2),
                (ends2_hbm, ends2),
                (widen_hbm, widen),
                (to_tiles_hbm, to_tiles),
                (from_tiles_hbm, from_tiles),
            )
        )
    ]
    for copy in inputs:
        copy.start()

    lane = lax.broadcasted_iota(jnp.int32, (8, 128), 1)
    sub = lax.broadcasted_iota(jnp.int32, (8, 128), 0)
    first = jnp.zeros((8, 128), jnp.int32)
    second = first
    third = first
    for a in range(16):
        mine = lane // 8 == a
        first = jnp.where(mine, first_s[a], first)
        second = jnp.where(mine, second_s[a], second)
        third = jnp.where(mine, third_s[a], third)
    energy = jnp.zeros((8, 128), F32)
    for p in range(NP):
        energy = jnp.where(sub == p, energy_s[p], energy)
    shift_x = (first - 4 - (dom % 2) * CX + 48) % 24
    shift_y = (second - 4 - (dom // 2 % 2) * CY + 64) % 32
    start_z = (third - 4 - (dom // 4) * CZ + 512) % 256
    cell_z = (start_z + lane % 8) % 256

    inputs[0].wait()
    swapped = proj_ref[...].T.reshape(64, 8, 128)
    lane3 = lax.broadcasted_iota(jnp.int32, (64, 8, 128), 2)
    sub3 = lax.broadcasted_iota(jnp.int32, (64, 8, 128), 1)
    for bit in (1, 2, 4):
        up = pltpu.roll(pltpu.roll(swapped, 8 - bit, 1), bit, 2)
        down = pltpu.roll(pltpu.roll(swapped, bit, 1), 128 - bit, 2)
        low_s = (sub3 // bit) % 2 == 0
        low_l = (lane3 // bit) % 2 == 0
        swapped = jnp.where(
            jnp.logical_and(low_s, jnp.logical_not(low_l)),
            up,
            jnp.where(jnp.logical_and(jnp.logical_not(low_s), low_l), down, swapped),
        )
    turned[...] = swapped.reshape(512, 128)

    fine = shift_y % 8
    tile_of = jnp.where(sub >= fine, shift_y // 8, (shift_y // 8 + 1) % 4)

    def place_y(i, carry):
        for p in range(NP):
            rows = turned[pl.ds(i * 64 + p, 8, stride=8), :]
            for bit in (1, 2, 4):
                rows = jnp.where((fine // bit) % 2 == 1, pltpu.roll(rows, bit, 0), rows)
            for half_y in range(2):
                across[i, p, pl.ds(8 * half_y, 8), :] = jnp.where(tile_of == half_y, rows, 0.0)
        return carry

    lax.fori_loop(0, 8, place_y, 0)

    def place_x(x, carry):
        hits = [shift_x == (x - i + 24) % 24 for i in range(8)]
        for p in range(NP):
            for half_y in range(2):
                total = jnp.zeros((8, 128), F32)
                for i in range(8):
                    total = jnp.where(hits[i], across[i, p, pl.ds(8 * half_y, 8), :], total)
                pxy[p, pl.ds(x * 16 + 8 * half_y, 8), :] = total
        return carry

    lax.fori_loop(0, CX, place_x, 0)

    zrow = lax.broadcasted_iota(jnp.int32, (128, 128), 0)
    onehot = jnp.where(zrow == jnp.broadcast_to(cell_z[0:1, :], (128, 128)), 1.0, 0.0)
    szf[0] = onehot.astype(BF16)
    szf[1] = onehot.T.astype(BF16)

    def partial_coefficients(source, k):
        high, low = split(source[k])
        picked = dot(high, szf[0]) + dot(low, szf[0])
        sums = [jnp.sum(picked * pxy[p], axis=0, keepdims=True) for p in range(NP)]
        return jnp.concatenate(sums, axis=0)

    def pack_coefficients(parts):
        return exact_dot(jnp.concatenate(parts, axis=1), join[...])

    def hold_coefficients(packed, slot):
        cmsg[slot] = packed
        crecv[slot, dom] = packed

    def send_coefficients(slot):
        copies = []
        for i in range(1, NDOM):
            copies.append(
                pltpu.make_async_remote_copy(
                    src_ref=cmsg.at[slot],
                    dst_ref=crecv.at[slot, dom],
                    send_sem=c_ssem.at[slot],
                    recv_sem=c_rsem.at[slot],
                    device_id=dom_peer(i),
                    device_id_type=MESH,
                )
            )
            copies[-1].start()

    def await_coefficients(slot):
        every = pltpu.make_async_remote_copy(
            src_ref=crecv.at[slot, pl.ds(0, NDOM - 1)],
            dst_ref=crecv.at[slot, pl.ds(0, NDOM - 1)],
            send_sem=c_ssem.at[slot],
            recv_sem=c_rsem.at[slot],
            device_id=dom_peer(1),
            device_id_type=MESH,
        )
        every.wait()
        total = crecv[slot, 0]
        for i in range(1, NDOM):
            total = total + crecv[slot, i]
        total = total * energy
        spread = exact_dot(total, part[...])
        for k in range(K):
            cfull[k] = spread[:, 128 * k : 128 * k + 128]

    def pack_halo(values, level, k):
        high = values.astype(BF16)
        xsend[level, k] = high
        ysend[level, k] = dot(pick_y[...], high).astype(BF16)
        packed = dot(high[0:32], pick_z[0:128, :])
        for g in range(1, 6):
            packed = packed + dot(high[32 * g : 32 * g + 32], pick_z[128 * g : 128 * g + 128, :])
        zsend[level, k] = packed.astype(BF16)

    def halo_copies(level, k):
        pairs = ((zsend, zrecv, 2), (ysend, yrecv, 1), (xsend, xrecv, 0))
        return [
            pltpu.make_async_remote_copy(
                src_ref=source.at[level, k],
                dst_ref=target.at[level, k],
                send_sem=halo_ssem.at[level, axis, k],
                recv_sem=halo_rsem.at[level, axis, k],
                device_id=partners[axis],
                device_id_type=MESH,
            )
            for source, target, axis in pairs
        ]

    def own_part(source, k):
        values = source[k]
        high, low = split(values)
        total = dot(own3[...], jnp.concatenate((high, high, low), axis=0))
        total = total + dot(jnp.concatenate((high, low, high), axis=1), line3[...])
        local = v_ref[...] + (3.0 * KINETIC * WEIGHTS[0] - CENTER)
        acc[k] = total + local * values

    def nonlocal_part(k):
        spread = pxy[0] * cfull[k, 0:1, :]
        for p in range(1, NP):
            spread = spread + pxy[p] * cfull[k, p : p + 1, :]
        high, low = split(spread)
        acc[k] = acc[k] + dot(high, szf[1]) + dot(low, szf[1])

    def halo_part(level, k):
        for copy in halo_copies(level, k):
            copy.wait_recv()
        got = jnp.concatenate((xrecv[level, k], yrecv[level, k]), axis=0)
        total = acc[k] + dot(both2[...], jnp.concatenate((got, got), axis=0))
        zgot = zrecv[level, k]
        ends = dot(jnp.concatenate((zgot, zgot), axis=1), ends2[...])
        flat = jnp.concatenate([ends[:, 128 * g : 128 * g + 128] for g in range(6)], axis=0)
        return total + flat

    inputs[1].wait()
    inputs[2].wait()
    parts = []
    high, low = split(x_ref[...].reshape(K * ROWS, CZ))
    picked = (dot(high, szf[0]) + dot(low, szf[0])).reshape(K, ROWS, CZ)
    for k in range(K):
        sums = [jnp.sum(picked[k] * pxy[p], axis=0, keepdims=True) for p in range(NP)]
        parts.append(jnp.concatenate(sums, axis=0))
    hold_coefficients(pack_coefficients(parts), 0)
    inputs[3].wait()
    inputs[4].wait()
    for k in range(K):
        pack_halo(x_ref[k], 0, k)
    rtmp[...] = jnp.zeros((16, 128), F32)
    wide = rot_ref[...].astype(F32)
    rtmp[0:5, :] = wide[:, 0:128]
    rtmp[5:10, :] = wide[:, 128:256]
    rtmp[10:15, 0:64] = wide[:, 256:320]
    rtile[...] = rtmp[...].astype(BF16)
    rall[orb] = rtile[...]

    pl.semaphore_wait(barrier, 31 + 7 + 2)
    send_coefficients(0)

    ring_copy = pltpu.make_async_remote_copy(
        src_ref=rtile,
        dst_ref=rother,
        send_sem=ring_ssem,
        recv_sem=ring_rsem,
        device_id=ring_peer(-1),
        device_id_type=MESH,
    )
    hands = [
        pltpu.make_async_remote_copy(
            src_ref=rother,
            dst_ref=rother,
            send_sem=hand_ssem.at[i],
            recv_sem=hand_rsem,
            device_id=dom_peer(i + 1),
            device_id_type=MESH,
        )
        for i in range(NDOM - 1)
    ]

    @pl.when(dom == 0)
    def _():
        ring_copy.start()

    for k in range(2):
        for copy in halo_copies(0, k):
            copy.start()

    def tile_copy(source, i, slot, wave):
        return pltpu.make_async_remote_copy(
            src_ref=source,
            dst_ref=rall.at[slot],
            send_sem=r_ssem.at[wave],
            recv_sem=r_rsem.at[wave],
            device_id=plane_peer(i),
            device_id_type=MESH,
        )

    def send_rows(i, carry):
        tile_copy(rtile, i, orb, 0).start()
        return carry

    lax.fori_loop(1, 32, send_rows, 0)

    @pl.when(dom == NDOM - 1)
    def _():
        ring_copy.wait_recv()
        for copy in hands:
            copy.start()

    for copy in inputs[5:]:
        copy.wait()
    for k in range(K):
        own_part(x_ref, k)
        if k + 2 < K:
            for copy in halo_copies(0, k):
                copy.wait_send()
            for copy in halo_copies(0, k + 2):
                copy.start()

    await_coefficients(0)

    parts = []
    for k in range(K):
        nonlocal_part(k)
        y1[k] = halo_part(0, k) * (1.0 / WIDTH)
        pack_halo(y1[k], 1, k)
        if k < AHEAD:
            for copy in halo_copies(1, k):
                copy.start()
        parts.append(partial_coefficients(y1, k))

    hold_coefficients(pack_coefficients(parts), 1)
    send_coefficients(1)
    for k in range(AHEAD, K):
        for copy in halo_copies(1, k):
            copy.start()

    @pl.when(dom == 0)
    def _():
        ring_copy.wait_send()

    @pl.when(dom == NDOM - 1)
    def _():
        for copy in hands:
            copy.wait_send()

    @pl.when(dom != NDOM - 1)
    def _():
        hands[0].wait_recv()

    orb_other = orb + 2 - 4 * zhi
    rall[orb_other] = rother[...]

    def send_other(i, carry):
        tile_copy(rother, i, orb_other, 1).start()
        return carry

    lax.fori_loop(1, 32, send_other, 0)

    for k in range(K):
        own_part(y1, k)

    await_coefficients(1)

    for k in range(K):
        nonlocal_part(k)
    for level in range(2):
        for k in range(K - 2 if level == 0 else 0, K):
            for copy in halo_copies(level, k):
                copy.wait_send()
    for k in range(K):
        fb[k] = (halo_part(1, k) * (2.0 / WIDTH) - x_ref[k]).astype(BF16)
    for g in range(4):
        rows = [fb[o, pl.ds((4 * r + g) * 16, 16), :] for o in range(K) for r in range(3)]
        tiles = dot(to_tiles[...], jnp.concatenate(rows, axis=0))
        fsend[16 * g : 16 * g + 16] = tiles.astype(BF16).reshape(16, 16, 128)

    for wave in range(2):
        every = tile_copy(rall.at[pl.ds(0, 31)], 1, pl.ds(0, 31), wave)
        every.wait()

    def exchange(source, target, q, wave):
        return pltpu.make_async_remote_copy(
            src_ref=source,
            dst_ref=target,
            send_sem=t_ssem.at[wave],
            recv_sem=t_rsem.at[wave],
            device_id=(dom, q),
            device_id_type=MESH,
        )

    core = orb % 2
    groups = (2 - 2 * zhi + core, 3 - 2 * zhi - core, 2 * zhi + 1 - core, 2 * zhi + core)
    place = orb // 4

    for index, group in enumerate(groups):

        def send_cells(j, carry):
            q = (place + j) % 16 * 4 + group
            exchange(fsend.at[q], frecv.at[orb], q, 0).start()
            return carry

        lax.fori_loop(1 if index == 3 else 0, 16, send_cells, 0)
    frecv[orb] = fsend[orb]

    rows_all = rall[...].reshape(1024, 128)
    row_e = lax.broadcasted_iota(jnp.int32, (256, 128), 0)
    lane_e = lax.broadcasted_iota(jnp.int32, (256, 128), 1)
    col_a = lax.broadcasted_iota(jnp.int32, (256, 1024), 1)
    row_b = lax.broadcasted_iota(jnp.int32, (256, 256), 0) % 16
    col_b = lax.broadcasted_iota(jnp.int32, (256, 256), 1) % 16
    same = row_b - 3 * (row_b * 11 // 32) == col_b - 3 * (col_b * 11 // 32)
    third_of = (col_a % 16) * 13 // 64

    def widen_rows(chunk, carry):
        member = row_e % 16
        target = 5 * (row_e // 16 * 4 + chunk) + member * 11 // 32
        target = jnp.where(member < 15, target, -1000)
        mixed = jnp.zeros((256, 1024), F32)
        for c in range(3):
            pick = jnp.where(lane_e == target - 128 * c, 1.0, 0.0).astype(BF16)
            part = lax.dot_general(
                pick, rows_all, (((1,), (1,)), ((), ())), preferred_element_type=F32
            )
            mixed = jnp.where(third_of == c, part, mixed)
        mixed = mixed.astype(BF16)
        for s in range(4):
            block = dot(mixed[:, 256 * s : 256 * s + 256], widen[...])
            rbig[pl.ds(chunk * 256, 256), pl.ds(256 * s, 256)] = jnp.where(same, block, 0.0).astype(BF16)
        return carry

    lax.fori_loop(0, 4, widen_rows, 0)

    every = exchange(fsend.at[pl.ds(0, 63)], frecv.at[pl.ds(0, 63)], orb, 0)
    every.wait()
    cells = frecv[...].reshape(1024, 128)
    for index, chunk in enumerate(groups):
        turned_cells = dot(rbig[pl.ds(pl.multiple_of(chunk * 256, 256), 256), :], cells)
        gsend[pl.ds(chunk * 16, 16)] = turned_cells.astype(BF16).reshape(16, 16, 128)

        def send_back(j, carry):
            other = (place + j) % 16
            q = other * 4 + chunk
            exchange(gsend.at[chunk * 16 + other], grecv.at[orb], q, 1).start()
            return carry

        lax.fori_loop(1 if index == 3 else 0, 16, send_back, 0)
    grecv[orb] = gsend[groups[3] * 16 + place]
    every = exchange(gsend.at[pl.ds(0, 63)], grecv.at[pl.ds(0, 63)], orb, 1)
    every.wait()
    for g in range(4):
        rows = dot(from_tiles[...], grecv[16 * g : 16 * g + 16].reshape(256, 128)).astype(BF16)
        for o in range(K):
            for r in range(3):
                m = 3 * o + r
                out_ref[o, pl.ds((4 * r + g) * 16, 16), :] = rows[16 * m : 16 * m + 16]


def body(
    orbitals, potential, projectors, projector_energy, atom_first, atom_second, atom_third, rotation
):
    consts = [jnp.asarray(t) for t in tables()]
    smem = pl.BlockSpec(memory_space=pltpu.SMEM)
    vmem = pl.BlockSpec(memory_space=pltpu.VMEM)
    anywhere = pl.BlockSpec(memory_space=pl.ANY)
    dma = pltpu.SemaphoreType.DMA
    placed = [((K, ROWS, CZ), F32), ((ROWS, CZ), F32), ((128, 512), F32)]
    placed += [(t.shape, BF16) for t in consts]
    scratch = [pltpu.VMEM(shape, kind) for shape, kind in placed] + [
        pltpu.VMEM((512, 128), F32),
        pltpu.VMEM((8, NP, 16, 128), F32),
        pltpu.VMEM((NP, ROWS, 128), F32),
        pltpu.VMEM((2, 128, 128), BF16),
        pltpu.VMEM((K, ROWS, CZ), F32),
        pltpu.VMEM((K, ROWS, CZ), F32),
        pltpu.VMEM((2, K, ROWS, CZ), BF16),
        pltpu.VMEM((2, K, 144, CZ), BF16),
        pltpu.VMEM((2, K, 32, CZ), BF16),
        pltpu.VMEM((2, K, ROWS, CZ), BF16),
        pltpu.VMEM((2, K, 144, CZ), BF16),
        pltpu.VMEM((2, K, 32, CZ), BF16),
        pltpu.VMEM((2, 8, 128), F32),
        pltpu.VMEM((2, NDOM, 8, 128), F32),
        pltpu.VMEM((K, 8, 128), F32),
        pltpu.VMEM((16, 128), F32),
        pltpu.VMEM((16, 128), BF16),
        pltpu.VMEM((16, 128), BF16),
        pltpu.VMEM((NORB_DEV, 16, 128), BF16),
        pltpu.VMEM((1024, 1024), BF16),
        pltpu.VMEM((K, ROWS, CZ), BF16),
        pltpu.VMEM((NORB_DEV, 16, 128), BF16),
        pltpu.VMEM((NORB_DEV, 16, 128), BF16),
        pltpu.VMEM((NORB_DEV, 16, 128), BF16),
        pltpu.VMEM((NORB_DEV, 16, 128), BF16),
        dma((2, 3, K)),
        dma((2, 3, K)),
        dma((2,)),
        dma((2,)),
        dma(()),
        dma(()),
        dma((NDOM - 1,)),
        dma(()),
        dma((2,)),
        dma((2,)),
        dma((2,)),
        dma((2,)),
        dma((14,)),
    ]
    result = pl.pallas_call(
        kernel,
        out_shape=jax.ShapeDtypeStruct((K, ROWS, CZ), BF16),
        in_specs=[smem] * 4 + [anywhere] * 3 + [vmem] + [anywhere] * len(consts),
        out_specs=vmem,
        scratch_shapes=scratch,
        compiler_params=pltpu.CompilerParams(
            collective_id=0, has_side_effects=True, vmem_limit_bytes=60 << 20
        ),
        name="filter_rotate",
    )(
        atom_first,
        atom_second,
        atom_third,
        projector_energy,
        orbitals.reshape(K, ROWS, CZ),
        potential.reshape(ROWS, CZ),
        projectors.reshape(128, 512),
        rotation,
        *consts,
    )
    return result.reshape((1, K, CX, CY, CZ))


def solution(mesh):
    return jax.shard_map(
        body,
        mesh=mesh,
        in_specs=(
            P("dom", "orb", None, None, None),
            P("dom", None, None, None),
            P(),
            P(),
            P(),
            P(),
            P(),
            P("orb", None),
        ),
        out_specs=P("dom", "orb", None, None, None),
        check_vma=False,
    )
```

```python
import functools

import jax
import jax.numpy as jnp
import numpy as np
from jax import lax
from jax.experimental import pallas as pl
from jax.experimental.pallas import tpu as pltpu
from jax.sharding import PartitionSpec as P

MESH = pl.DeviceIdType.MESH
F32 = jnp.float32
BF16 = jnp.bfloat16

K, CX, CY, CZ = 5, 12, 16, 128
ROWS = CX * CY
NP = 8
NDOM, NORB_DEV = 8, 64
REACH = 6
AHEAD = 1
WEIGHTS = (
    -5369.0 / 1800.0,
    12.0 / 7.0,
    -15.0 / 56.0,
    10.0 / 189.0,
    -1.0 / 112.0,
    2.0 / 1925.0,
    -1.0 / 16632.0,
)
KINETIC = -8.0
CENTER = 120.0
WIDTH = 110.0


def halves(matrix):
    high = matrix.astype(np.float32).astype(jnp.bfloat16)
    low = (matrix - high.astype(np.float64)).astype(np.float32).astype(jnp.bfloat16)
    return high, low


def hop(distance):
    distance = abs(distance)
    return KINETIC * WEIGHTS[distance] if 1 <= distance <= REACH else 0.0


@functools.cache
def tables():
    own = np.zeros((CX, CY, CX, CY))
    for x in range(CX):
        for y in range(CY):
            for other in range(CX):
                own[x, y, other, y] += hop(x - other)
            for other in range(CY):
                own[x, y, x, other] += hop(y - other)
    own_high, own_low = halves(own.reshape(ROWS, ROWS))
    own3 = np.concatenate((own_high, own_low, own_high), axis=1)

    near = np.zeros((CX, CY, CX, CY))
    for x in range(CX):
        for other in range(CX):
            near[x, np.arange(CY), other, np.arange(CY)] = hop(other + CX - x) + hop(other - CX - x)
    kept = list(range(REACH)) + list(range(CY - REACH, CY))
    side = np.zeros((CX, CY, CX, 2 * REACH))
    pick_y = np.zeros((CX, 2 * REACH, CX, CY))
    for slot, row in enumerate(kept):
        for x in range(CX):
            pick_y[x, slot, x, row] = 1.0
            for y in range(CY):
                side[x, y, x, slot] = hop(row + CY - y) + hop(row - CY - y)
    both = np.concatenate((near.reshape(ROWS, ROWS), side.reshape(ROWS, 12 * CX)), axis=1)
    both_high, both_low = halves(both)
    both2 = np.concatenate((both_high, both_low), axis=1)
    pick_y = pick_y.reshape(12 * CX, ROWS).astype(jnp.bfloat16)

    line = np.array([[hop(z - other) for other in range(CZ)] for z in range(CZ)])
    line_high, line_low = halves(line)
    line3 = np.concatenate((line_high, line_high, line_low), axis=0)

    pick_z = np.zeros((6, CZ, CZ))
    ends = np.zeros((CZ, 6, CZ))
    lanes = list(range(REACH)) + list(range(CZ - REACH, CZ))
    for g in range(6):
        for slot, lane in enumerate(lanes):
            pick_z[g, lane, 12 * g + slot] = 1.0
            for z in range(CZ):
                ends[12 * g + slot, g, z] = hop(lane + CZ - z) + hop(lane - CZ - z)
    ends_high, ends_low = halves(ends.reshape(CZ, 6 * CZ))
    ends2 = np.concatenate((ends_high, ends_low), axis=0)
    pick_z = pick_z.reshape(6 * CZ, CZ).astype(jnp.bfloat16)

    to_tiles = np.zeros((16, 16, 15, 16))
    for q in range(16):
        for m in range(15):
            to_tiles[q, m, m, q] = 1.0
    to_tiles = to_tiles.reshape(256, 240).astype(jnp.bfloat16)
    from_tiles = np.ascontiguousarray(to_tiles.T)

    widen = np.zeros((16, 16, 16, 16))
    for s in range(16):
        for c in range(3):
            for o in range(K):
                for r in range(3):
                    widen[s, 5 * c + o, s, 3 * o + r] = 1.0
    widen = widen.reshape(256, 256).astype(jnp.bfloat16)
    join = np.zeros((K, 128, 128))
    for k in range(K):
        for lane in range(128):
            join[k, lane, 16 * k + lane // 8] = 1.0
    part = np.ascontiguousarray(join.transpose(2, 0, 1)).reshape(128, K * 128).astype(jnp.bfloat16)
    join = join.reshape(K * 128, 128).astype(jnp.bfloat16)
    return own3, both2, line3, ends2, pick_y, pick_z, to_tiles, from_tiles, widen, join, part


def split(values):
    high = values.astype(BF16)
    low = (values - high.astype(F32)).astype(BF16)
    return high, low


def dot(a, b):
    return jnp.dot(a, b, preferred_element_type=F32)


def thirds(values):
    high = values.astype(BF16)
    middle, low = split(values - high.astype(F32))
    return jnp.concatenate((high, middle, low), axis=0)


def exact_dot(values, onehot):
    parts = dot(thirds(values), onehot)
    return parts[0:8] + parts[8:16] + parts[16:24]


def kernel(
    first_s, second_s, third_s, energy_s,
    x_hbm, v_hbm, proj_hbm, rot_ref,
    own3_hbm, both2_hbm, line3_hbm, ends2_hbm, pick_y_hbm, pick_z_hbm, to_tiles_hbm, from_tiles_hbm, widen_hbm, join_hbm, part_hbm,
    out_ref,
    x_ref, v_ref, proj_ref, own3, both2, line3, ends2, pick_y, pick_z, to_tiles, from_tiles, widen, join, part,
    turned, across, pxy, szf, y1, acc,
    xsend, ysend, zsend, xrecv, yrecv, zrecv,
    cmsg, crecv, cfull,
    rtmp, rtile, rother, rall,
    rbig, fb, fsend, frecv, gsend, grecv,
    halo_ssem, halo_rsem, c_ssem, c_rsem, ring_ssem, ring_rsem, hand_ssem, hand_rsem, r_ssem, r_rsem, t_ssem, t_rsem, in_sem,
):
    dom = lax.axis_index("dom")
    orb = lax.axis_index("orb")
    zhi = (orb // 2) % 2
    lane_u = (orb // 4) * 2 + orb % 2

    def plane_peer(i):
        u = (lane_u + i) % 32
        return (dom, (u // 2) * 4 + zhi * 2 + u % 2)

    def dom_peer(i):
        return ((dom + i) % NDOM, orb)

    def ring_peer(step):
        z = (zhi * 8 + dom + step + 16) % 16
        return (z % 8, orb - zhi * 2 + (z // 8) * 2)

    partners = (
        (dom + 1 - 2 * (dom % 2), orb),
        (dom + 2 - 4 * ((dom // 2) % 2), orb),
        (dom + 4 - 8 * (dom // 4), orb),
    )

    barrier = pltpu.get_barrier_semaphore()

    def greet_plane(i, carry):
        pl.semaphore_signal(barrier, inc=1, device_id=plane_peer(i), device_id_type=MESH)
        return carry

    def greet_dom(i, carry):
        pl.semaphore_signal(barrier, inc=1, device_id=dom_peer(i), device_id_type=MESH)
        return carry

    lax.fori_loop(1, NDOM, greet_dom, 0)
    for step in (1, -1):
        pl.semaphore_signal(barrier, inc=1, device_id=ring_peer(step), device_id_type=MESH)
    lax.fori_loop(1, 32, greet_plane, 0)

    inputs = [
        pltpu.make_async_copy(source, target, in_sem.at[index])
        for index, (source, target) in enumerate(
            (
                (proj_hbm, proj_ref),
                (x_hbm, x_ref),
                (join_hbm, join),
                (pick_y_hbm, pick_y),
                (pick_z_hbm, pick_z),
                (own3_hbm, own3),
                (line3_hbm, line3),
                (part_hbm, part),
                (v_hbm, v_ref),
                (both2_hbm, both2),
                (ends2_hbm, ends2),
                (widen_hbm, widen),
                (to_tiles_hbm, to_tiles),
                (from_tiles_hbm, from_tiles),
            )
        )
    ]
    for copy in inputs:
        copy.start()

    lane = lax.broadcasted_iota(jnp.int32, (8, 128), 1)
    sub = lax.broadcasted_iota(jnp.int32, (8, 128), 0)
    first = jnp.zeros((8, 128), jnp.int32)
    second = first
    third = first
    for a in range(16):
        mine = lane // 8 == a
        first = jnp.where(mine, first_s[a], first)
        second = jnp.where(mine, second_s[a], second)
        third = jnp.where(mine, third_s[a], third)
    energy = jnp.zeros((8, 128), F32)
    for p in range(NP):
        energy = jnp.where(sub == p, energy_s[p], energy)
    shift_x = (first - 4 - (dom % 2) * CX + 48) % 24
    shift_y = (second - 4 - (dom // 2 % 2) * CY + 64) % 32
    start_z = (third - 4 - (dom // 4) * CZ + 512) % 256
    cell_z = (start_z + lane % 8) % 256

    inputs[0].wait()
    swapped = proj_ref[...].T.reshape(64, 8, 128)
    lane3 = lax.broadcasted_iota(jnp.int32, (64, 8, 128), 2)
    sub3 = lax.broadcasted_iota(jnp.int32, (64, 8, 128), 1)
    for bit in (1, 2, 4):
        up = pltpu.roll(pltpu.roll(swapped, 8 - bit, 1), bit, 2)
        down = pltpu.roll(pltpu.roll(swapped, bit, 1), 128 - bit, 2)
        low_s = (sub3 // bit) % 2 == 0
        low_l = (lane3 // bit) % 2 == 0
        swapped = jnp.where(
            jnp.logical_and(low_s, jnp.logical_not(low_l)),
            up,
            jnp.where(jnp.logical_and(jnp.logical_not(low_s), low_l), down, swapped),
        )
    turned[...] = swapped.reshape(512, 128)

    fine = shift_y % 8
    tile_of = jnp.where(sub >= fine, shift_y // 8, (shift_y // 8 + 1) % 4)

    def place_y(i, carry):
        for p in range(NP):
            rows = turned[pl.ds(i * 64 + p, 8, stride=8), :]
            for bit in (1, 2, 4):
                rows = jnp.where((fine // bit) % 2 == 1, pltpu.roll(rows, bit, 0), rows)
            for half_y in range(2):
                across[i, p, pl.ds(8 * half_y, 8), :] = jnp.where(tile_of == half_y, rows, 0.0)
        return carry

    lax.fori_loop(0, 8, place_y, 0)

    def place_x(x, carry):
        hits = [shift_x == (x - i + 24) % 24 for i in range(8)]
        for p in range(NP):
            for half_y in range(2):
                total = jnp.zeros((8, 128), F32)
                for i in range(8):
                    total = jnp.where(hits[i], across[i, p, pl.ds(8 * half_y, 8), :], total)
                pxy[p, pl.ds(x * 16 + 8 * half_y, 8), :] = total
        return carry

    lax.fori_loop(0, CX, place_x, 0)

    zrow = lax.broadcasted_iota(jnp.int32, (128, 128), 0)
    onehot = jnp.where(zrow == jnp.broadcast_to(cell_z[0:1, :], (128, 128)), 1.0, 0.0)
    szf[0] = onehot.astype(BF16)
    szf[1] = onehot.T.astype(BF16)

    def partial_coefficients(source, k):
        high, low = split(source[k])
        picked = dot(high, szf[0]) + dot(low, szf[0])
        sums = [jnp.sum(picked * pxy[p], axis=0, keepdims=True) for p in range(NP)]
        return jnp.concatenate(sums, axis=0)

    def pack_coefficients(parts):
        return exact_dot(jnp.concatenate(parts, axis=1), join[...])

    def hold_coefficients(packed, slot):
        cmsg[slot] = packed
        crecv[slot, dom] = packed

    def send_coefficients(slot):
        copies = []
        for i in range(1, NDOM):
            copies.append(
                pltpu.make_async_remote_copy(
                    src_ref=cmsg.at[slot],
                    dst_ref=crecv.at[slot, dom],
                    send_sem=c_ssem.at[slot],
                    recv_sem=c_rsem.at[slot],
                    device_id=dom_peer(i),
                    device_id_type=MESH,
                )
            )
            copies[-1].start()

    def await_coefficients(slot):
        every = pltpu.make_async_remote_copy(
            src_ref=crecv.at[slot, pl.ds(0, NDOM - 1)],
            dst_ref=crecv.at[slot, pl.ds(0, NDOM - 1)],
            send_sem=c_ssem.at[slot],
            recv_sem=c_rsem.at[slot],
            device_id=dom_peer(1),
            device_id_type=MESH,
        )
        every.wait()
        total = crecv[slot, 0]
        for i in range(1, NDOM):
            total = total + crecv[slot, i]
        total = total * energy
        spread = exact_dot(total, part[...])
        for k in range(K):
            cfull[k] = spread[:, 128 * k : 128 * k + 128]

    def pack_halo(values, level, k):
        high = values.astype(BF16)
        xsend[level, k] = high
        ysend[level, k] = dot(pick_y[...], high).astype(BF16)
        packed = dot(high[0:32], pick_z[0:128, :])
        for g in range(1, 6):
            packed = packed + dot(high[32 * g : 32 * g + 32], pick_z[128 * g : 128 * g + 128, :])
        zsend[level, k] = packed.astype(BF16)

    def halo_copies(level, k):
        pairs = ((zsend, zrecv, 2), (ysend, yrecv, 1), (xsend, xrecv, 0))
        return [
            pltpu.make_async_remote_copy(
                src_ref=source.at[level, k],
                dst_ref=target.at[level, k],
                send_sem=halo_ssem.at[level, axis, k],
                recv_sem=halo_rsem.at[level, axis, k],
                device_id=partners[axis],
                device_id_type=MESH,
            )
            for source, target, axis in pairs
        ]

    def own_part(source, k):
        values = source[k]
        high, low = split(values)
        total = dot(own3[...], jnp.concatenate((high, high, low), axis=0))
        total = total + dot(jnp.concatenate((high, low, high), axis=1), line3[...])
        local = v_ref[...] + (3.0 * KINETIC * WEIGHTS[0] - CENTER)
        acc[k] = total + local * values

    def nonlocal_part(k):
        spread = pxy[0] * cfull[k, 0:1, :]
        for p in range(1, NP):
            spread = spread + pxy[p] * cfull[k, p : p + 1, :]
        high, low = split(spread)
        acc[k] = acc[k] + dot(high, szf[1]) + dot(low, szf[1])

    def halo_part(level, k):
        for copy in halo_copies(level, k):
            copy.wait_recv()
        got = jnp.concatenate((xrecv[level, k], yrecv[level, k]), axis=0)
        total = acc[k] + dot(both2[...], jnp.concatenate((got, got), axis=0))
        zgot = zrecv[level, k]
        ends = dot(jnp.concatenate((zgot, zgot), axis=1), ends2[...])
        flat = jnp.concatenate([ends[:, 128 * g : 128 * g + 128] for g in range(6)], axis=0)
        return total + flat

    inputs[1].wait()
    inputs[2].wait()
    parts = []
    high, low = split(x_ref[...].reshape(K * ROWS, CZ))
    picked = (dot(high, szf[0]) + dot(low, szf[0])).reshape(K, ROWS, CZ)
    for k in range(K):
        sums = [jnp.sum(picked[k] * pxy[p], axis=0, keepdims=True) for p in range(NP)]
        parts.append(jnp.concatenate(sums, axis=0))
    hold_coefficients(pack_coefficients(parts), 0)
    inputs[3].wait()
    inputs[4].wait()
    for k in range(K):
        pack_halo(x_ref[k], 0, k)
    rtmp[...] = jnp.zeros((16, 128), F32)
    wide = rot_ref[...].astype(F32)
    rtmp[0:5, :] = wide[:, 0:128]
    rtmp[5:10, :] = wide[:, 128:256]
    rtmp[10:15, 0:64] = wide[:, 256:320]
    rtile[...] = rtmp[...].astype(BF16)
    rall[orb] = rtile[...]

    pl.semaphore_wait(barrier, 31 + 7 + 2)
    send_coefficients(0)

    ring_copy = pltpu.make_async_remote_copy(
        src_ref=rtile,
        dst_ref=rother,
        send_sem=ring_ssem,
        recv_sem=ring_rsem,
        device_id=ring_peer(-1),
        device_id_type=MESH,
    )
    hands = [
        pltpu.make_async_remote_copy(
            src_ref=rother,
            dst_ref=rother,
            send_sem=hand_ssem.at[i],
            recv_sem=hand_rsem,
            device_id=dom_peer(i + 1),
            device_id_type=MESH,
        )
        for i in range(NDOM - 1)
    ]

    @pl.when(dom == 0)
    def _():
        ring_copy.start()

    for k in range(2):
        for copy in halo_copies(0, k):
            copy.start()

    def tile_copy(source, i, slot, wave):
        return pltpu.make_async_remote_copy(
            src_ref=source,
            dst_ref=rall.at[slot],
            send_sem=r_ssem.at[wave],
            recv_sem=r_rsem.at[wave],
            device_id=plane_peer(i),
            device_id_type=MESH,
        )

    def send_rows(i, carry):
        tile_copy(rtile, i, orb, 0).start()
        return carry

    lax.fori_loop(1, 32, send_rows, 0)

    @pl.when(dom == NDOM - 1)
    def _():
        ring_copy.wait_recv()
        for copy in hands:
            copy.start()

    for copy in inputs[5:]:
        copy.wait()
    for k in range(K):
        own_part(x_ref, k)
        if k + 2 < K:
            for copy in halo_copies(0, k):
                copy.wait_send()
            for copy in halo_copies(0, k + 2):
                copy.start()

    await_coefficients(0)

    parts = []
    for k in range(K):
        nonlocal_part(k)
        y1[k] = halo_part(0, k) * (1.0 / WIDTH)
        pack_halo(y1[k], 1, k)
        if k < AHEAD:
            for copy in halo_copies(1, k):
                copy.start()
        parts.append(partial_coefficients(y1, k))

    hold_coefficients(pack_coefficients(parts), 1)
    send_coefficients(1)
    for k in range(AHEAD, K):
        for copy in halo_copies(1, k):
            copy.start()

    @pl.when(dom == 0)
    def _():
        ring_copy.wait_send()

    @pl.when(dom == NDOM - 1)
    def _():
        for copy in hands:
            copy.wait_send()

    @pl.when(dom != NDOM - 1)
    def _():
        hands[0].wait_recv()

    orb_other = orb + 2 - 4 * zhi
    rall[orb_other] = rother[...]

    def send_other(i, carry):
        tile_copy(rother, i, orb_other, 1).start()
        return carry

    lax.fori_loop(1, 32, send_other, 0)

    for k in range(K):
        own_part(y1, k)

    await_coefficients(1)

    for k in range(K):
        nonlocal_part(k)
    for k in range(K):
        fb[k] = (halo_part(1, k) * (2.0 / WIDTH) - x_ref[k]).astype(BF16)
    for g in range(4):
        rows = [fb[o, pl.ds((4 * r + g) * 16, 16), :] for o in range(K) for r in range(3)]
        tiles = dot(to_tiles[...], jnp.concatenate(rows, axis=0))
        fsend[16 * g : 16 * g + 16] = tiles.astype(BF16).reshape(16, 16, 128)

    for wave in range(2):
        every = tile_copy(rall.at[pl.ds(0, 31)], 1, pl.ds(0, 31), wave)
        every.wait()

    def exchange(source, target, q, wave):
        return pltpu.make_async_remote_copy(
            src_ref=source,
            dst_ref=target,
            send_sem=t_ssem.at[wave],
            recv_sem=t_rsem.at[wave],
            device_id=(dom, q),
            device_id_type=MESH,
        )

    core = orb % 2
    groups = (2 - 2 * zhi + core, 3 - 2 * zhi - core, 2 * zhi + 1 - core, 2 * zhi + core)
    place = orb // 4

    for index, group in enumerate(groups):

        def send_cells(j, carry):
            q = (place + j) % 16 * 4 + group
            exchange(fsend.at[q], frecv.at[orb], q, 0).start()
            return carry

        lax.fori_loop(1 if index == 3 else 0, 16, send_cells, 0)
    frecv[orb] = fsend[orb]

    for level in range(2):
        for k in range(K - 2 if level == 0 else 0, K):
            for copy in halo_copies(level, k):
                copy.wait_send()

    rows_all = rall[...].reshape(1024, 128)
    row_e = lax.broadcasted_iota(jnp.int32, (256, 128), 0)
    lane_e = lax.broadcasted_iota(jnp.int32, (256, 128), 1)
    col_a = lax.broadcasted_iota(jnp.int32, (256, 1024), 1)
    row_b = lax.broadcasted_iota(jnp.int32, (256, 256), 0) % 16
    col_b = lax.broadcasted_iota(jnp.int32, (256, 256), 1) % 16
    same = row_b - 3 * (row_b * 11 // 32) == col_b - 3 * (col_b * 11 // 32)
    third_of = (col_a % 16) * 13 // 64

    def widen_rows(chunk, carry):
        member = row_e % 16
        target = 5 * (row_e // 16 * 4 + chunk) + member * 11 // 32
        target = jnp.where(member < 15, target, -1000)
        mixed = jnp.zeros((256, 1024), F32)
        for c in range(3):
            pick = jnp.where(lane_e == target - 128 * c, 1.0, 0.0).astype(BF16)
            part = lax.dot_general(
                pick, rows_all, (((1,), (1,)), ((), ())), preferred_element_type=F32
            )
            mixed = jnp.where(third_of == c, part, mixed)
        mixed = mixed.astype(BF16)
        for s in range(4):
            block = dot(mixed[:, 256 * s : 256 * s + 256], widen[...])
            rbig[pl.ds(chunk * 256, 256), pl.ds(256 * s, 256)] = jnp.where(same, block, 0.0).astype(BF16)
        return carry

    lax.fori_loop(0, 4, widen_rows, 0)

    every = exchange(fsend.at[pl.ds(0, 63)], frecv.at[pl.ds(0, 63)], orb, 0)
    every.wait()
    cells = frecv[...].reshape(1024, 128)
    for index, chunk in enumerate(groups):
        turned_cells = dot(rbig[pl.ds(pl.multiple_of(chunk * 256, 256), 256), :], cells)
        gsend[pl.ds(chunk * 16, 16)] = turned_cells.astype(BF16).reshape(16, 16, 128)

        def send_back(j, carry):
            other = (place + j) % 16
            q = other * 4 + chunk
            exchange(gsend.at[chunk * 16 + other], grecv.at[orb], q, 1).start()
            return carry

        lax.fori_loop(1 if index == 3 else 0, 16, send_back, 0)
    grecv[orb] = gsend[groups[3] * 16 + place]
    every = exchange(gsend.at[pl.ds(0, 63)], grecv.at[pl.ds(0, 63)], orb, 1)
    every.wait()
    for g in range(4):
        rows = dot(from_tiles[...], grecv[16 * g : 16 * g + 16].reshape(256, 128)).astype(BF16)
        for o in range(K):
            for r in range(3):
                m = 3 * o + r
                out_ref[o, pl.ds((4 * r + g) * 16, 16), :] = rows[16 * m : 16 * m + 16]


def body(
    orbitals, potential, projectors, projector_energy, atom_first, atom_second, atom_third, rotation
):
    consts = [jnp.asarray(t) for t in tables()]
    smem = pl.BlockSpec(memory_space=pltpu.SMEM)
    vmem = pl.BlockSpec(memory_space=pltpu.VMEM)
    anywhere = pl.BlockSpec(memory_space=pl.ANY)
    dma = pltpu.SemaphoreType.DMA
    placed = [((K, ROWS, CZ), F32), ((ROWS, CZ), F32), ((128, 512), F32)]
    placed += [(t.shape, BF16) for t in consts]
    scratch = [pltpu.VMEM(shape, kind) for shape, kind in placed] + [
        pltpu.VMEM((512, 128), F32),
        pltpu.VMEM((8, NP, 16, 128), F32),
        pltpu.VMEM((NP, ROWS, 128), F32),
        pltpu.VMEM((2, 128, 128), BF16),
        pltpu.VMEM((K, ROWS, CZ), F32),
        pltpu.VMEM((K, ROWS, CZ), F32),
        pltpu.VMEM((2, K, ROWS, CZ), BF16),
        pltpu.VMEM((2, K, 144, CZ), BF16),
        pltpu.VMEM((2, K, 32, CZ), BF16),
        pltpu.VMEM((2, K, ROWS, CZ), BF16),
        pltpu.VMEM((2, K, 144, CZ), BF16),
        pltpu.VMEM((2, K, 32, CZ), BF16),
        pltpu.VMEM((2, 8, 128), F32),
        pltpu.VMEM((2, NDOM, 8, 128), F32),
        pltpu.VMEM((K, 8, 128), F32),
        pltpu.VMEM((16, 128), F32),
        pltpu.VMEM((16, 128), BF16),
        pltpu.VMEM((16, 128), BF16),
        pltpu.VMEM((NORB_DEV, 16, 128), BF16),
        pltpu.VMEM((1024, 1024), BF16),
        pltpu.VMEM((K, ROWS, CZ), BF16),
        pltpu.VMEM((NORB_DEV, 16, 128), BF16),
        pltpu.VMEM((NORB_DEV, 16, 128), BF16),
        pltpu.VMEM((NORB_DEV, 16, 128), BF16),
        pltpu.VMEM((NORB_DEV, 16, 128), BF16),
        dma((2, 3, K)),
        dma((2, 3, K)),
        dma((2,)),
        dma((2,)),
        dma(()),
        dma(()),
        dma((NDOM - 1,)),
        dma(()),
        dma((2,)),
        dma((2,)),
        dma((2,)),
        dma((2,)),
        dma((14,)),
    ]
    result = pl.pallas_call(
        kernel,
        out_shape=jax.ShapeDtypeStruct((K, ROWS, CZ), BF16),
        in_specs=[smem] * 4 + [anywhere] * 3 + [vmem] + [anywhere] * len(consts),
        out_specs=vmem,
        scratch_shapes=scratch,
        compiler_params=pltpu.CompilerParams(
            collective_id=0, has_side_effects=True, vmem_limit_bytes=60 << 20
        ),
        name="filter_rotate",
    )(
        atom_first,
        atom_second,
        atom_third,
        projector_energy,
        orbitals.reshape(K, ROWS, CZ),
        potential.reshape(ROWS, CZ),
        projectors.reshape(128, 512),
        rotation,
        *consts,
    )
    return result.reshape((1, K, CX, CY, CZ))


def solution(mesh):
    return jax.shard_map(
        body,
        mesh=mesh,
        in_specs=(
            P("dom", "orb", None, None, None),
            P("dom", None, None, None),
            P(),
            P(),
            P(),
            P(),
            P(),
            P("orb", None),
        ),
        out_specs=P("dom", "orb", None, None, None),
        check_vma=False,
    )
```

```python
import functools

import jax
import jax.numpy as jnp
import numpy as np
from jax import lax
from jax.experimental import pallas as pl
from jax.experimental.pallas import tpu as pltpu
from jax.sharding import PartitionSpec as P

MESH = pl.DeviceIdType.MESH
F32 = jnp.float32
BF16 = jnp.bfloat16

K, CX, CY, CZ = 5, 12, 16, 128
ROWS = CX * CY
NP = 8
NDOM, NORB_DEV = 8, 64
REACH = 6
AHEAD = 1
WEIGHTS = (
    -5369.0 / 1800.0,
    12.0 / 7.0,
    -15.0 / 56.0,
    10.0 / 189.0,
    -1.0 / 112.0,
    2.0 / 1925.0,
    -1.0 / 16632.0,
)
KINETIC = -8.0
CENTER = 120.0
WIDTH = 110.0


def halves(matrix):
    high = matrix.astype(np.float32).astype(jnp.bfloat16)
    low = (matrix - high.astype(np.float64)).astype(np.float32).astype(jnp.bfloat16)
    return high, low


def hop(distance):
    distance = abs(distance)
    return KINETIC * WEIGHTS[distance] if 1 <= distance <= REACH else 0.0


@functools.cache
def tables():
    own = np.zeros((CX, CY, CX, CY))
    for x in range(CX):
        for y in range(CY):
            for other in range(CX):
                own[x, y, other, y] += hop(x - other)
            for other in range(CY):
                own[x, y, x, other] += hop(y - other)
    own_high, own_low = halves(own.reshape(ROWS, ROWS))
    own3 = np.concatenate((own_high, own_low, own_high), axis=1)

    near = np.zeros((CX, CY, CX, CY))
    for x in range(CX):
        for other in range(CX):
            near[x, np.arange(CY), other, np.arange(CY)] = hop(other + CX - x) + hop(other - CX - x)
    kept = list(range(REACH)) + list(range(CY - REACH, CY))
    side = np.zeros((CX, CY, CX, 2 * REACH))
    pick_y = np.zeros((CX, 2 * REACH, CX, CY))
    for slot, row in enumerate(kept):
        for x in range(CX):
            pick_y[x, slot, x, row] = 1.0
            for y in range(CY):
                side[x, y, x, slot] = hop(row + CY - y) + hop(row - CY - y)
    both = np.concatenate((near.reshape(ROWS, ROWS), side.reshape(ROWS, 12 * CX)), axis=1)
    both_high, both_low = halves(both)
    both2 = np.concatenate((both_high, both_low), axis=1)
    pick_y = pick_y.reshape(12 * CX, ROWS).astype(jnp.bfloat16)

    line = np.array([[hop(z - other) for other in range(CZ)] for z in range(CZ)])
    line_high, line_low = halves(line)
    line3 = np.concatenate((line_high, line_high, line_low), axis=0)

    pick_z = np.zeros((6, CZ, CZ))
    ends = np.zeros((CZ, 6, CZ))
    lanes = list(range(REACH)) + list(range(CZ - REACH, CZ))
    for g in range(6):
        for slot, lane in enumerate(lanes):
            pick_z[g, lane, 12 * g + slot] = 1.0
            for z in range(CZ):
                ends[12 * g + slot, g, z] = hop(lane + CZ - z) + hop(lane - CZ - z)
    ends_high, ends_low = halves(ends.reshape(CZ, 6 * CZ))
    ends2 = np.concatenate((ends_high, ends_low), axis=0)
    pick_z = pick_z.reshape(6 * CZ, CZ).astype(jnp.bfloat16)

    to_tiles = np.zeros((16, 16, 15, 16))
    for q in range(16):
        for m in range(15):
            to_tiles[q, m, m, q] = 1.0
    to_tiles = to_tiles.reshape(256, 240).astype(jnp.bfloat16)
    from_tiles = np.ascontiguousarray(to_tiles.T)

    widen = np.zeros((16, 16, 16, 16))
    for s in range(16):
        for c in range(3):
            for o in range(K):
                for r in range(3):
                    widen[s, 5 * c + o, s, 3 * o + r] = 1.0
    widen = widen.reshape(256, 256).astype(jnp.bfloat16)
    join = np.zeros((K, 128, 128))
    for k in range(K):
        for lane in range(128):
            join[k, lane, 16 * k + lane // 8] = 1.0
    part = np.ascontiguousarray(join.transpose(2, 0, 1)).reshape(128, K * 128).astype(jnp.bfloat16)
    join = join.reshape(K * 128, 128).astype(jnp.bfloat16)
    return own3, both2, line3, ends2, pick_y, pick_z, to_tiles, from_tiles, widen, join, part


def split(values):
    high = values.astype(BF16)
    low = (values - high.astype(F32)).astype(BF16)
    return high, low


def dot(a, b):
    return jnp.dot(a, b, preferred_element_type=F32)


def thirds(values):
    high = values.astype(BF16)
    middle, low = split(values - high.astype(F32))
    return jnp.concatenate((high, middle, low), axis=0)


def exact_dot(values, onehot):
    parts = dot(thirds(values), onehot)
    return parts[0:8] + parts[8:16] + parts[16:24]


def kernel(
    first_s, second_s, third_s, energy_s,
    x_hbm, v_hbm, proj_hbm, rot_ref,
    own3_hbm, both2_hbm, line3_hbm, ends2_hbm, pick_y_hbm, pick_z_hbm, to_tiles_hbm, from_tiles_hbm, widen_hbm, join_hbm, part_hbm,
    out_ref,
    x_ref, v_ref, proj_ref, own3, both2, line3, ends2, pick_y, pick_z, to_tiles, from_tiles, widen, join, part,
    turned, across, pxy, szf, y1, acc,
    xsend, ysend, zsend, xrecv, yrecv, zrecv,
    cmsg, crecv, cfull,
    rtmp, rtile, rother, rall,
    rbig, fb, fsend, frecv, gsend, grecv,
    halo_ssem, halo_rsem, c_ssem, c_rsem, ring_ssem, ring_rsem, hand_ssem, hand_rsem, r_ssem, r_rsem, t_ssem, t_rsem, in_sem,
):
    dom = lax.axis_index("dom")
    orb = lax.axis_index("orb")
    zhi = (orb // 2) % 2
    lane_u = (orb // 4) * 2 + orb % 2

    def plane_peer(i):
        u = (lane_u + i) % 32
        return (dom, (u // 2) * 4 + zhi * 2 + u % 2)

    def dom_peer(i):
        return ((dom + i) % NDOM, orb)

    def ring_peer(step):
        z = (zhi * 8 + dom + step + 16) % 16
        return (z % 8, orb - zhi * 2 + (z // 8) * 2)

    partners = (
        (dom + 1 - 2 * (dom % 2), orb),
        (dom + 2 - 4 * ((dom // 2) % 2), orb),
        (dom + 4 - 8 * (dom // 4), orb),
    )

    barrier = pltpu.get_barrier_semaphore()

    def greet_plane(i, carry):
        pl.semaphore_signal(barrier, inc=1, device_id=plane_peer(i), device_id_type=MESH)
        return carry

    def greet_dom(i, carry):
        pl.semaphore_signal(barrier, inc=1, device_id=dom_peer(i), device_id_type=MESH)
        return carry

    lax.fori_loop(1, NDOM, greet_dom, 0)
    for step in (1, -1):
        pl.semaphore_signal(barrier, inc=1, device_id=ring_peer(step), device_id_type=MESH)
    lax.fori_loop(1, 32, greet_plane, 0)

    inputs = [
        pltpu.make_async_copy(source, target, in_sem.at[index])
        for index, (source, target) in enumerate(
            (
                (proj_hbm, proj_ref),
                (x_hbm, x_ref),
                (join_hbm, join),
                (pick_y_hbm, pick_y),
                (pick_z_hbm, pick_z),
                (own3_hbm, own3),
                (line3_hbm, line3),
                (part_hbm, part),
                (v_hbm, v_ref),
                (both2_hbm, both2),
                (ends2_hbm, ends2),
                (widen_hbm, widen),
                (to_tiles_hbm, to_tiles),
                (from_tiles_hbm, from_tiles),
            )
        )
    ]
    for copy in inputs:
        copy.start()

    lane = lax.broadcasted_iota(jnp.int32, (8, 128), 1)
    sub = lax.broadcasted_iota(jnp.int32, (8, 128), 0)
    first = jnp.zeros((8, 128), jnp.int32)
    second = first
    third = first
    for a in range(16):
        mine = lane // 8 == a
        first = jnp.where(mine, first_s[a], first)
        second = jnp.where(mine, second_s[a], second)
        third = jnp.where(mine, third_s[a], third)
    energy = jnp.zeros((8, 128), F32)
    for p in range(NP):
        energy = jnp.where(sub == p, energy_s[p], energy)
    shift_x = (first - 4 - (dom % 2) * CX + 48) % 24
    shift_y = (second - 4 - (dom // 2 % 2) * CY + 64) % 32
    start_z = (third - 4 - (dom // 4) * CZ + 512) % 256
    cell_z = (start_z + lane % 8) % 256

    inputs[0].wait()
    swapped = proj_ref[...].T.reshape(64, 8, 128)
    lane3 = lax.broadcasted_iota(jnp.int32, (64, 8, 128), 2)
    sub3 = lax.broadcasted_iota(jnp.int32, (64, 8, 128), 1)
    for bit in (1, 2, 4):
        up = pltpu.roll(pltpu.roll(swapped, 8 - bit, 1), bit, 2)
        down = pltpu.roll(pltpu.roll(swapped, bit, 1), 128 - bit, 2)
        low_s = (sub3 // bit) % 2 == 0
        low_l = (lane3 // bit) % 2 == 0
        swapped = jnp.where(
            jnp.logical_and(low_s, jnp.logical_not(low_l)),
            up,
            jnp.where(jnp.logical_and(jnp.logical_not(low_s), low_l), down, swapped),
        )
    turned[...] = swapped.reshape(512, 128)

    fine = shift_y % 8
    tile_of = jnp.where(sub >= fine, shift_y // 8, (shift_y // 8 + 1) % 4)

    def place_y(i, carry):
        for p in range(NP):
            rows = turned[pl.ds(i * 64 + p, 8, stride=8), :]
            for bit in (1, 2, 4):
                rows = jnp.where((fine // bit) % 2 == 1, pltpu.roll(rows, bit, 0), rows)
            for half_y in range(2):
                across[i, p, pl.ds(8 * half_y, 8), :] = jnp.where(tile_of == half_y, rows, 0.0)
        return carry

    lax.fori_loop(0, 8, place_y, 0)

    def place_x(x, carry):
        hits = [shift_x == (x - i + 24) % 24 for i in range(8)]
        for p in range(NP):
            for half_y in range(2):
                total = jnp.zeros((8, 128), F32)
                for i in range(8):
                    total = jnp.where(hits[i], across[i, p, pl.ds(8 * half_y, 8), :], total)
                pxy[p, pl.ds(x * 16 + 8 * half_y, 8), :] = total
        return carry

    lax.fori_loop(0, CX, place_x, 0)

    zrow = lax.broadcasted_iota(jnp.int32, (128, 128), 0)
    onehot = jnp.where(zrow == jnp.broadcast_to(cell_z[0:1, :], (128, 128)), 1.0, 0.0)
    szf[0] = onehot.astype(BF16)
    szf[1] = onehot.T.astype(BF16)

    def partial_coefficients(source, k):
        high, low = split(source[k])
        picked = dot(high, szf[0]) + dot(low, szf[0])
        sums = [jnp.sum(picked * pxy[p], axis=0, keepdims=True) for p in range(NP)]
        return jnp.concatenate(sums, axis=0)

    def pack_coefficients(parts):
        return exact_dot(jnp.concatenate(parts, axis=1), join[...])

    def hold_coefficients(packed, slot):
        cmsg[slot] = packed
        crecv[slot, dom] = packed

    def send_coefficients(slot):
        copies = []
        for i in range(1, NDOM):
            copies.append(
                pltpu.make_async_remote_copy(
                    src_ref=cmsg.at[slot],
                    dst_ref=crecv.at[slot, dom],
                    send_sem=c_ssem.at[slot],
                    recv_sem=c_rsem.at[slot],
                    device_id=dom_peer(i),
                    device_id_type=MESH,
                )
            )
            copies[-1].start()

    def await_coefficients(slot):
        every = pltpu.make_async_remote_copy(
            src_ref=crecv.at[slot, pl.ds(0, NDOM - 1)],
            dst_ref=crecv.at[slot, pl.ds(0, NDOM - 1)],
            send_sem=c_ssem.at[slot],
            recv_sem=c_rsem.at[slot],
            device_id=dom_peer(1),
            device_id_type=MESH,
        )
        every.wait()
        total = crecv[slot, 0]
        for i in range(1, NDOM):
            total = total + crecv[slot, i]
        total = total * energy
        spread = exact_dot(total, part[...])
        for k in range(K):
            cfull[k] = spread[:, 128 * k : 128 * k + 128]

    def pack_halo(values, level, k):
        high = values.astype(BF16)
        xsend[level, k] = high
        ysend[level, k] = dot(pick_y[...], high).astype(BF16)
        packed = dot(high[0:32], pick_z[0:128, :])
        for g in range(1, 6):
            packed = packed + dot(high[32 * g : 32 * g + 32], pick_z[128 * g : 128 * g + 128, :])
        zsend[level, k] = packed.astype(BF16)

    def halo_copies(level, k):
        pairs = ((zsend, zrecv, 2), (ysend, yrecv, 1), (xsend, xrecv, 0))
        return [
            pltpu.make_async_remote_copy(
                src_ref=source.at[level, k],
                dst_ref=target.at[level, k],
                send_sem=halo_ssem.at[level, axis, k],
                recv_sem=halo_rsem.at[level, axis, k],
                device_id=partners[axis],
                device_id_type=MESH,
            )
            for source, target, axis in pairs
        ]

    def own_part(source, k):
        values = source[k]
        high, low = split(values)
        total = dot(own3[...], jnp.concatenate((high, high, low), axis=0))
        total = total + dot(jnp.concatenate((high, low, high), axis=1), line3[...])
        local = v_ref[...] + (3.0 * KINETIC * WEIGHTS[0] - CENTER)
        acc[k] = total + local * values

    def nonlocal_part(k):
        spread = pxy[0] * cfull[k, 0:1, :]
        for p in range(1, NP):
            spread = spread + pxy[p] * cfull[k, p : p + 1, :]
        high, low = split(spread)
        acc[k] = acc[k] + dot(high, szf[1]) + dot(low, szf[1])

    def halo_part(level, k):
        for copy in halo_copies(level, k):
            copy.wait_recv()
        got = jnp.concatenate((xrecv[level, k], yrecv[level, k]), axis=0)
        total = acc[k] + dot(both2[...], jnp.concatenate((got, got), axis=0))
        zgot = zrecv[level, k]
        ends = dot(jnp.concatenate((zgot, zgot), axis=1), ends2[...])
        flat = jnp.concatenate([ends[:, 128 * g : 128 * g + 128] for g in range(6)], axis=0)
        return total + flat

    inputs[1].wait()
    inputs[2].wait()
    parts = []
    high, low = split(x_ref[...].reshape(K * ROWS, CZ))
    picked = (dot(high, szf[0]) + dot(low, szf[0])).reshape(K, ROWS, CZ)
    for k in range(K):
        sums = [jnp.sum(picked[k] * pxy[p], axis=0, keepdims=True) for p in range(NP)]
        parts.append(jnp.concatenate(sums, axis=0))
    hold_coefficients(pack_coefficients(parts), 0)
    inputs[3].wait()
    inputs[4].wait()
    for k in range(K):
        pack_halo(x_ref[k], 0, k)
    rtmp[...] = jnp.zeros((16, 128), F32)
    wide = rot_ref[...].astype(F32)
    rtmp[0:5, :] = wide[:, 0:128]
    rtmp[5:10, :] = wide[:, 128:256]
    rtmp[10:15, 0:64] = wide[:, 256:320]
    rtile[...] = rtmp[...].astype(BF16)
    rall[orb] = rtile[...]

    pl.semaphore_wait(barrier, 31 + 7 + 2)
    send_coefficients(0)

    ring_copy = pltpu.make_async_remote_copy(
        src_ref=rtile,
        dst_ref=rother,
        send_sem=ring_ssem,
        recv_sem=ring_rsem,
        device_id=ring_peer(-1),
        device_id_type=MESH,
    )
    hands = [
        pltpu.make_async_remote_copy(
            src_ref=rother,
            dst_ref=rother,
            send_sem=hand_ssem.at[i],
            recv_sem=hand_rsem,
            device_id=dom_peer(i + 1),
            device_id_type=MESH,
        )
        for i in range(NDOM - 1)
    ]

    @pl.when(dom == 0)
    def _():
        ring_copy.start()

    for k in range(2):
        for copy in halo_copies(0, k):
            copy.start()

    def tile_copy(source, i, slot, wave):
        return pltpu.make_async_remote_copy(
            src_ref=source,
            dst_ref=rall.at[slot],
            send_sem=r_ssem.at[wave],
            recv_sem=r_rsem.at[wave],
            device_id=plane_peer(i),
            device_id_type=MESH,
        )

    def send_rows(i, carry):
        tile_copy(rtile, i, orb, 0).start()
        return carry

    lax.fori_loop(1, 32, send_rows, 0)

    @pl.when(dom == NDOM - 1)
    def _():
        ring_copy.wait_recv()
        for copy in hands:
            copy.start()

    for copy in inputs[5:]:
        copy.wait()
    for k in range(K):
        own_part(x_ref, k)
        if k + 2 < K:
            for copy in halo_copies(0, k):
                copy.wait_send()
            for copy in halo_copies(0, k + 2):
                copy.start()

    await_coefficients(0)

    parts = []
    for k in range(K):
        nonlocal_part(k)
        y1[k] = halo_part(0, k) * (1.0 / WIDTH)
        pack_halo(y1[k], 1, k)
        if k < AHEAD:
            for copy in halo_copies(1, k):
                copy.start()
        parts.append(partial_coefficients(y1, k))

    hold_coefficients(pack_coefficients(parts), 1)
    send_coefficients(1)
    for k in range(AHEAD, K):
        for copy in halo_copies(1, k):
            copy.start()

    for k in range(K):
        own_part(y1, k)

    @pl.when(dom == 0)
    def _():
        ring_copy.wait_send()

    @pl.when(dom == NDOM - 1)
    def _():
        for copy in hands:
            copy.wait_send()

    @pl.when(dom != NDOM - 1)
    def _():
        hands[0].wait_recv()

    orb_other = orb + 2 - 4 * zhi
    rall[orb_other] = rother[...]

    def send_other(i, carry):
        tile_copy(rother, i, orb_other, 1).start()
        return carry

    lax.fori_loop(1, 32, send_other, 0)

    await_coefficients(1)

    for k in range(K):
        nonlocal_part(k)
    for level in range(2):
        for k in range(K - 2 if level == 0 else 0, K):
            for copy in halo_copies(level, k):
                copy.wait_send()
    for k in range(K):
        fb[k] = (halo_part(1, k) * (2.0 / WIDTH) - x_ref[k]).astype(BF16)
    for g in range(4):
        rows = [fb[o, pl.ds((4 * r + g) * 16, 16), :] for o in range(K) for r in range(3)]
        tiles = dot(to_tiles[...], jnp.concatenate(rows, axis=0))
        fsend[16 * g : 16 * g + 16] = tiles.astype(BF16).reshape(16, 16, 128)

    for wave in range(2):
        every = tile_copy(rall.at[pl.ds(0, 31)], 1, pl.ds(0, 31), wave)
        every.wait()

    def exchange(source, target, q, wave):
        return pltpu.make_async_remote_copy(
            src_ref=source,
            dst_ref=target,
            send_sem=t_ssem.at[wave],
            recv_sem=t_rsem.at[wave],
            device_id=(dom, q),
            device_id_type=MESH,
        )

    core = orb % 2
    groups = (2 - 2 * zhi + core, 3 - 2 * zhi - core, 2 * zhi + 1 - core, 2 * zhi + core)
    place = orb // 4

    for index, group in enumerate(groups):

        def send_cells(j, carry):
            q = (place + j) % 16 * 4 + group
            exchange(fsend.at[q], frecv.at[orb], q, 0).start()
            return carry

        lax.fori_loop(1 if index == 3 else 0, 16, send_cells, 0)
    frecv[orb] = fsend[orb]

    rows_all = rall[...].reshape(1024, 128)
    row_e = lax.broadcasted_iota(jnp.int32, (256, 128), 0)
    lane_e = lax.broadcasted_iota(jnp.int32, (256, 128), 1)
    col_a = lax.broadcasted_iota(jnp.int32, (256, 1024), 1)
    row_b = lax.broadcasted_iota(jnp.int32, (256, 256), 0) % 16
    col_b = lax.broadcasted_iota(jnp.int32, (256, 256), 1) % 16
    same = row_b - 3 * (row_b * 11 // 32) == col_b - 3 * (col_b * 11 // 32)
    third_of = (col_a % 16) * 13 // 64

    def widen_rows(chunk, carry):
        member = row_e % 16
        target = 5 * (row_e // 16 * 4 + chunk) + member * 11 // 32
        target = jnp.where(member < 15, target, -1000)
        mixed = jnp.zeros((256, 1024), F32)
        for c in range(3):
            pick = jnp.where(lane_e == target - 128 * c, 1.0, 0.0).astype(BF16)
            part = lax.dot_general(
                pick, rows_all, (((1,), (1,)), ((), ())), preferred_element_type=F32
            )
            mixed = jnp.where(third_of == c, part, mixed)
        mixed = mixed.astype(BF16)
        for s in range(4):
            block = dot(mixed[:, 256 * s : 256 * s + 256], widen[...])
            rbig[pl.ds(chunk * 256, 256), pl.ds(256 * s, 256)] = jnp.where(same, block, 0.0).astype(BF16)
        return carry

    lax.fori_loop(0, 4, widen_rows, 0)

    every = exchange(fsend.at[pl.ds(0, 63)], frecv.at[pl.ds(0, 63)], orb, 0)
    every.wait()
    cells = frecv[...].reshape(1024, 128)
    for index, chunk in enumerate(groups):
        turned_cells = dot(rbig[pl.ds(pl.multiple_of(chunk * 256, 256), 256), :], cells)
        gsend[pl.ds(chunk * 16, 16)] = turned_cells.astype(BF16).reshape(16, 16, 128)

        def send_back(j, carry):
            other = (place + j) % 16
            q = other * 4 + chunk
            exchange(gsend.at[chunk * 16 + other], grecv.at[orb], q, 1).start()
            return carry

        lax.fori_loop(1 if index == 3 else 0, 16, send_back, 0)
    grecv[orb] = gsend[groups[3] * 16 + place]
    every = exchange(gsend.at[pl.ds(0, 63)], grecv.at[pl.ds(0, 63)], orb, 1)
    every.wait()
    for g in range(4):
        rows = dot(from_tiles[...], grecv[16 * g : 16 * g + 16].reshape(256, 128)).astype(BF16)
        for o in range(K):
            for r in range(3):
                m = 3 * o + r
                out_ref[o, pl.ds((4 * r + g) * 16, 16), :] = rows[16 * m : 16 * m + 16]


def body(
    orbitals, potential, projectors, projector_energy, atom_first, atom_second, atom_third, rotation
):
    consts = [jnp.asarray(t) for t in tables()]
    smem = pl.BlockSpec(memory_space=pltpu.SMEM)
    vmem = pl.BlockSpec(memory_space=pltpu.VMEM)
    anywhere = pl.BlockSpec(memory_space=pl.ANY)
    dma = pltpu.SemaphoreType.DMA
    placed = [((K, ROWS, CZ), F32), ((ROWS, CZ), F32), ((128, 512), F32)]
    placed += [(t.shape, BF16) for t in consts]
    scratch = [pltpu.VMEM(shape, kind) for shape, kind in placed] + [
        pltpu.VMEM((512, 128), F32),
        pltpu.VMEM((8, NP, 16, 128), F32),
        pltpu.VMEM((NP, ROWS, 128), F32),
        pltpu.VMEM((2, 128, 128), BF16),
        pltpu.VMEM((K, ROWS, CZ), F32),
        pltpu.VMEM((K, ROWS, CZ), F32),
        pltpu.VMEM((2, K, ROWS, CZ), BF16),
        pltpu.VMEM((2, K, 144, CZ), BF16),
        pltpu.VMEM((2, K, 32, CZ), BF16),
        pltpu.VMEM((2, K, ROWS, CZ), BF16),
        pltpu.VMEM((2, K, 144, CZ), BF16),
        pltpu.VMEM((2, K, 32, CZ), BF16),
        pltpu.VMEM((2, 8, 128), F32),
        pltpu.VMEM((2, NDOM, 8, 128), F32),
        pltpu.VMEM((K, 8, 128), F32),
        pltpu.VMEM((16, 128), F32),
        pltpu.VMEM((16, 128), BF16),
        pltpu.VMEM((16, 128), BF16),
        pltpu.VMEM((NORB_DEV, 16, 128), BF16),
        pltpu.VMEM((1024, 1024), BF16),
        pltpu.VMEM((K, ROWS, CZ), BF16),
        pltpu.VMEM((NORB_DEV, 16, 128), BF16),
        pltpu.VMEM((NORB_DEV, 16, 128), BF16),
        pltpu.VMEM((NORB_DEV, 16, 128), BF16),
        pltpu.VMEM((NORB_DEV, 16, 128), BF16),
        dma((2, 3, K)),
        dma((2, 3, K)),
        dma((2,)),
        dma((2,)),
        dma(()),
        dma(()),
        dma((NDOM - 1,)),
        dma(()),
        dma((2,)),
        dma((2,)),
        dma((2,)),
        dma((2,)),
        dma((14,)),
    ]
    result = pl.pallas_call(
        kernel,
        out_shape=jax.ShapeDtypeStruct((K, ROWS, CZ), BF16),
        in_specs=[smem] * 4 + [anywhere] * 3 + [vmem] + [anywhere] * len(consts),
        out_specs=vmem,
        scratch_shapes=scratch,
        compiler_params=pltpu.CompilerParams(
            collective_id=0, has_side_effects=True, vmem_limit_bytes=60 << 20
        ),
        name="filter_rotate",
    )(
        atom_first,
        atom_second,
        atom_third,
        projector_energy,
        orbitals.reshape(K, ROWS, CZ),
        potential.reshape(ROWS, CZ),
        projectors.reshape(128, 512),
        rotation,
        *consts,
    )
    return result.reshape((1, K, CX, CY, CZ))


def solution(mesh):
    return jax.shard_map(
        body,
        mesh=mesh,
        in_specs=(
            P("dom", "orb", None, None, None),
            P("dom", None, None, None),
            P(),
            P(),
            P(),
            P(),
            P(),
            P("orb", None),
        ),
        out_specs=P("dom", "orb", None, None, None),
        check_vma=False,
    )
```
